32 devices in a mesh: dp: 8 (over z, y), tensor: 4 (over x, core).
Axes of the slice: x: 2, y: 2, z: 4, core: 2. Of those that a mesh axis runs over, the one named last changes fastest.
Arguments:
- hidden: bfloat16 [1024, 7168], P('dp', 'tensor'), may hold values from -6 to 6
- hash_rows: int32 [1024, 4], P('dp', 'tensor'), may hold values from 0 to 8191, as said below
- memory_table: bfloat16 [8192, 896], P(('dp', 'tensor')), may hold values from -6 to 6
- key_weight: bfloat16 [3584, 7168], P(None, 'tensor'), may hold values from -0.09375 to 0.09375
- value_weight: bfloat16 [3584, 7168], P(None, 'tensor'), may hold values from -0.09375 to 0.09375
- hidden_gain: float32 [7168], P('tensor'), may hold values from 0.1 to 1.9
- key_gain: float32 [7168], P('tensor'), may hold values from 0.1 to 1.9
Outputs:
- joined: bfloat16 [1024, 7168], P('dp', 'tensor')
The draws below stay inside these ranges and needn't reach their ends.
Inputs may be any that keep to these rules, and one draw needn't show every extreme that they name: `hash_rows`: row r lies in the block of 256 rows held by device r // 256 of dp+tensor. Of the lookups that one device holds (128 requests of its dp group times its 4 / 4 heads), at most 8 fall into any one device's block, and in every draw some device's block receives exactly 8 from every device.
All inputs are finite; a program needn't handle non-finite values.
Results may differ from the reference program's by a relative error of at most 0.0014.
Values may be sent and summed in bfloat16 or wider, within the bound.
A program may use at most 64 MiB of HBM per device.

```python
import jax
import jax.numpy as jnp
from jax import lax

D = 7168
HEADW = 896
HEADS = 4
REQ = 128
ROWS_DEV = 256
MEM = 3584
TOKENS = 1024
ROWS = 8192
CAP = 8
N_DP = 8
N_TENSOR = 4


def draw_hash_rows(key, part):
    owners = N_DP * N_TENSOR
    per_device = REQ * (HEADS // N_TENSOR)
    slot_count = owners * CAP
    hot_owner = jax.random.randint(jax.random.fold_in(key, 11), (), 0, owners)
    slot_owner = jnp.arange(slot_count, dtype=jnp.int32) // CAP
    slot_rank = jnp.arange(slot_count, dtype=jnp.int32) % CAP

    def one_device(device_index):
        device_key = jax.random.fold_in(jax.random.fold_in(key, 23), device_index)
        shuffle_order = jax.random.permutation(jax.random.fold_in(device_key, 1), slot_count)
        placing = jnp.zeros((slot_count,), jnp.int32).at[shuffle_order].set(jnp.arange(slot_count, dtype=jnp.int32))
        priority = jnp.where(slot_owner == hot_owner, slot_rank - CAP, placing)
        chosen = jnp.argsort(priority, stable=True)[:per_device]
        picked = slot_owner[chosen]
        shuffled = picked[jax.random.permutation(jax.random.fold_in(device_key, 2), per_device)]
        local_rows = jax.random.randint(jax.random.fold_in(device_key, 3), (per_device,), 0, ROWS_DEV)
        return shuffled * ROWS_DEV + local_rows
    drawn = jax.vmap(one_device)(jnp.arange(owners, dtype=jnp.int32))
    blocks = drawn.reshape(N_DP, N_TENSOR, REQ, HEADS // N_TENSOR)
    return jnp.transpose(blocks, (0, 2, 1, 3)).reshape(N_DP * REQ, HEADS).astype(jnp.int32)


def block_levels(rng, dims, split, least, largest):
    loudness, own = 1.0, jax.random.fold_in(rng, 6)
    for dim, blocks in split:
        draws = jnp.exp(jax.random.uniform(jax.random.fold_in(own, dim), (blocks,), jnp.float32, least / len(split), largest / len(split)))
        loudness = loudness * jnp.repeat(draws, dims[dim] // blocks).reshape([-1 if axis == dim else 1 for axis in range(len(dims))])
    return loudness


def gaussian(stream_key, extent, scale, bound, cuts=(), kind=jnp.bfloat16):
    entries = jax.random.normal(stream_key, extent, jnp.float32) * scale
    if len(cuts) > 0:
        entries = block_levels(stream_key, extent, cuts, -0.22, 0.18) * entries
    return jnp.clip(entries, min=-bound, max=bound).astype(kind)


def setup_inputs(seed: int = 0) -> dict:
    key_of = jax.random.split(jax.random.key(seed), 8)
    hidden = gaussian(key_of[0], (TOKENS, D), 1.0, 6.0, ((0, 8), (1, 4)))
    hash_rows = draw_hash_rows(jax.random.fold_in(key_of[7], 71), 0)
    memory_table = gaussian(key_of[2], (ROWS, HEADW), 1.0, 6.0, ((0, 32),))
    key_weight = gaussian(key_of[3], (MEM, D), MEM ** -0.5, 0.09375, ((1, 4),))
    value_weight = gaussian(key_of[4], (MEM, D), MEM ** -0.5, 0.09375, ((1, 4),))
    hidden_gain = jnp.clip(1.0 + 0.18 * jax.random.normal(key_of[5], (D,), jnp.float32), 0.1, 1.9)
    key_gain = jnp.clip(1.0 + 0.18 * jax.random.normal(key_of[6], (D,), jnp.float32), 0.1, 1.9)
    return {"hidden": hidden, "hash_rows": hash_rows, "memory_table": memory_table, "key_weight": key_weight, "value_weight": value_weight, "hidden_gain": hidden_gain, "key_gain": key_gain}


epsilon = 1e-06

def reference(hidden, hash_rows, memory_table, key_weight, value_weight, hidden_gain, key_gain):

    def group_output(arrays):
        hidden_rows, index_rows = arrays
        memory = memory_table[index_rows].reshape(index_rows.shape[0], MEM)
        key = jnp.dot(memory, key_weight, preferred_element_type=jnp.float32)
        projected = jnp.dot(memory, value_weight, preferred_element_type=jnp.float32)
        hidden_float = hidden_rows.astype(jnp.float32)
        hidden_power = lax.optimization_barrier(jnp.mean(hidden_float * hidden_float, axis=1))
        key_power = lax.optimization_barrier(jnp.mean(key * key, axis=1))
        crossing = lax.optimization_barrier(jnp.sum(hidden_float * hidden_gain * key * key_gain, axis=1))
        agreement = crossing * lax.rsqrt(hidden_power + epsilon) * lax.rsqrt(key_power + epsilon)
        gate_value = jax.nn.sigmoid(agreement / jnp.sqrt(jnp.float32(D)))
        return (hidden_float + gate_value[:, None] * projected).astype(jnp.bfloat16)
    outputs = lax.map(group_output, (hidden.reshape(N_DP, REQ, D), hash_rows.reshape(N_DP, REQ, HEADS)))
    return outputs.reshape(N_DP * REQ, D)
```

```python
import functools
import math

import jax
import jax.numpy as jnp
from jax import lax
from jax.experimental import pallas as pl
from jax.experimental.pallas import tpu as pltpu
from jax.sharding import PartitionSpec as P

MESH = pl.DeviceIdType.MESH
epsilon = 1e-06
F32, BF16 = jnp.float32, jnp.bfloat16
LANES = 128


def dot(a, b):
    return jnp.dot(a, b, preferred_element_type=F32)


def kernel(groups, heads, slots, sizes, ids_hbm, hg_hbm, kg_hbm, table_hbm, hidden_hbm, wk_hbm, wv_hbm, out_ref,
           ids, hg, kg, table, hidden, scaled, wk, wv, lists_out, lists_in, sending, rows, place, mem, acc_k, acc_v,
           stats, local_sem, list_send, list_recv, row_send, row_recv, pass_send, pass_recv, stat_send, stat_recv):
    me_p, me_t = lax.axis_index("dp"), lax.axis_index("tensor")
    me = me_p * heads + me_t
    owners = groups * heads
    held, width = table.shape
    requests, columns = hidden.shape
    model = columns * heads
    part = 256 if columns % 256 == 0 else 128
    starts = [sum(sizes[:c]) for c in range(len(sizes))]
    last = len(sizes) - 1

    def here(source, target, sem):
        return pltpu.make_async_copy(source, target, sem)

    def there(source, target, send, recv, p, t):
        return pltpu.make_async_remote_copy(
            src_ref=source, dst_ref=target, send_sem=send, recv_sem=recv,
            device_id={"dp": p, "tensor": t}, device_id_type=MESH)

    def peer(i):
        j = owners - i
        return me_p ^ lax.div(j, heads), me_t ^ lax.rem(j, heads)

    barrier = pltpu.get_barrier_semaphore()

    @pl.loop(1, owners)
    def _(i):
        p, t = peer(i)
        pl.semaphore_signal(barrier, inc=1, device_id={"dp": p, "tensor": t}, device_id_type=MESH)

    ids_copy = here(ids_hbm, ids, local_sem.at[0])
    table_copy = here(table_hbm, table, local_sem.at[1])
    hidden_copy = here(hidden_hbm, hidden, local_sem.at[2])
    hg_copy = here(hg_hbm, hg, local_sem.at[3])
    kg_copy = here(kg_hbm, kg, local_sem.at[4])
    for copy in (ids_copy, table_copy, hidden_copy, hg_copy, kg_copy):
        copy.start()
    for start, size in zip(starts, sizes):
        for k, (source, target) in enumerate(((wk_hbm, wk), (wv_hbm, wv))):
            for h in range(heads):
                here(source.at[pl.ds(h * width + start, size), :],
                     target.at[pl.ds(heads * start + h * size, size), :], local_sem.at[5 + k]).start()

    ids_copy.wait()
    sub = lax.broadcasted_iota(jnp.int32, (requests, requests), 0)
    lane = lax.broadcasted_iota(jnp.int32, (requests, requests), 1)
    numbers = ids[0].astype(F32)
    owner_row = jnp.floor((numbers + 0.5) * (1.0 / held))
    local_row = numbers - owner_row * held
    owner = jnp.broadcast_to(owner_row, (requests, requests))
    column = jnp.sum(jnp.where(sub == lane, owner, 0.0), axis=1, keepdims=True)
    inside = jnp.sum(jnp.where(sub == lane, jnp.broadcast_to(local_row, (requests, requests)), 0.0), axis=1, keepdims=True)
    rank = jnp.sum(jnp.where((owner == column) & (lane < sub), 1.0, 0.0), axis=1, keepdims=True)
    spots = lax.broadcasted_iota(jnp.int32, (requests, owners * slots), 1).astype(F32)
    place[...] = jnp.where(spots == column * slots + rank, 1.0, 0.0).astype(BF16)
    whose = lax.broadcasted_iota(jnp.int32, (owners, requests), 0).astype(F32)
    belongs = jnp.where(whose == owner_row, 1.0, 0.0).astype(BF16)
    slot_lane = lax.broadcasted_iota(jnp.int32, (requests, LANES), 1).astype(F32)
    ranked = jnp.where(slot_lane == rank, inside, 0.0).astype(BF16)
    lists_out[...] = dot(belongs, ranked).reshape(owners, 1, LANES)

    here(lists_out.at[me], lists_in.at[me], list_recv.at[0]).start()
    pl.semaphore_wait(barrier, owners - 1)

    @pl.loop(1, owners)
    def _(i):
        p, t = peer(i)
        there(lists_out.at[p * heads + t], lists_in.at[me], list_send.at[0], list_recv.at[0], p, t).start()

    hidden_copy.wait()
    hg_copy.wait()
    kg_copy.wait()
    hidden_squares = jnp.zeros((requests, LANES), F32)
    for c in range(columns // LANES):
        cols = slice(c * LANES, (c + 1) * LANES)
        value = hidden[:, cols].astype(F32)
        hidden_squares += value * value
        scaled[:, cols] = value * (hg[cols] * kg[cols]).reshape(1, LANES)
    hidden_squares = jnp.sum(hidden_squares, axis=1, keepdims=True)

    table_copy.wait()
    there(lists_out, lists_in, list_send.at[0], list_recv.at[0], me_p, me_t).wait_recv()
    shape = (owners, slots, LANES)
    diagonal = lax.broadcasted_iota(jnp.int32, shape, 1) == lax.broadcasted_iota(jnp.int32, shape, 2)
    wanted = jnp.sum(jnp.where(diagonal, jnp.broadcast_to(lists_in[...], shape), 0.0), axis=2, keepdims=True)
    wanted = wanted.reshape(owners * slots, 1)
    choose = jnp.where(
        lax.broadcasted_iota(jnp.int32, (owners * slots, held), 1).astype(F32) == wanted, 1.0, 0.0).astype(BF16)

    for c, (start, size) in enumerate(zip(starts, sizes)):
        cols = pl.ds(start, size)
        block = dot(choose, table[:, cols])
        sending[:, :, cols] = block.reshape(owners, slots, size).astype(BF16)
        here(sending.at[me, :, cols], rows.at[me, :, cols], row_recv.at[c]).start()

        @pl.loop(1, owners)
        def _(i):
            p, t = peer(i)
            there(sending.at[p * heads + t, :, cols], rows.at[me, :, cols], row_send.at[0], row_recv.at[c], p, t).start()

    def blocks(c):
        return pl.ds(starts[c] // LANES, sizes[c] // LANES)

    def share(c, h, m):
        return lambda n: there(mem.at[h, blocks(c)], mem.at[h, blocks(c)], pass_send.at[0],
                               pass_recv.at[c * (heads - 1) + n - 1], me_p, me_t ^ m)

    def arrived(c, n):
        return there(mem.at[me_t ^ n, blocks(c)], mem.at[me_t ^ n, blocks(c)], pass_send.at[0],
                     pass_recv.at[c * (heads - 1) + n - 1], me_p, me_t ^ n)

    def relayed(c):
        return c != last

    def compact(c):
        cols = pl.ds(starts[c], sizes[c])
        there(sending.at[:, :, cols], rows.at[:, :, cols], row_send.at[0], row_recv.at[c], me_p, me_t).wait_recv()
        mine = dot(place[...], rows[:, :, cols].reshape(owners * slots, sizes[c])).astype(BF16)
        for b in range(sizes[c] // LANES):
            mem[me_t, starts[c] // LANES + b] = mine[:, b * LANES:(b + 1) * LANES]
        for m in list(range(2, heads)) + [1]:
            if m % 2 == 0 or m == 1 or not relayed(c):
                share(c, me_t, m)(m).start()

    def relay(c):
        if relayed(c):
            for m in range(2, heads, 2):
                arrived(c, m).wait_recv()
                share(c, me_t ^ m, 1)(m | 1).start()

    def operand(c, base, count):
        b0, nb = starts[c] // LANES, sizes[c] // LANES
        return jnp.concatenate([mem[base + h, b0 + b] for h in range(count) for b in range(nb)], axis=1)

    def multiply(c, w, acc, base, count):
        x = operand(c, base, count)
        first = heads * starts[c] + base * sizes[c]
        if not isinstance(first, int):
            first = pl.multiple_of(first, LANES)
        depth = pl.ds(first, count * sizes[c])
        for n in range(columns // part):
            cols = pl.ds(n * part, part)
            value = dot(x, w[depth, cols])
            acc[:, cols] = value if c == 0 else acc[:, cols] + value

    def gathered(c):
        for m in range(1, heads):
            if not relayed(c) or m % 2:
                arrived(c, m).wait_recv()

    def product(c):
        gathered(c)
        multiply(c, wk, acc_k, 0, heads)
        multiply(c, wv, acc_v, 0, heads)

    for c in range(last + 1):
        compact(c)
        if c >= 1:
            relay(c - 1)
        if c == 1:
            here(wk_hbm, wk, local_sem.at[5]).wait()
            here(wv_hbm, wv, local_sem.at[6]).wait()
        if c >= 2:
            product(c - 2)
    product(last - 1)

    pair = me_t - lax.rem(me_t, 2)
    arrived(last, 1).wait_recv()
    multiply(last, wk, acc_k, pair, 2)
    for m in range(2, heads, 2):
        arrived(last, m).wait_recv()
        arrived(last, m + 1).wait_recv()
        multiply(last, wk, acc_k, pair ^ m, 2)

    key_squares = jnp.zeros((requests, LANES), F32)
    crossing = jnp.zeros((requests, LANES), F32)
    for c in range(columns // LANES):
        cols = slice(c * LANES, (c + 1) * LANES)
        key = acc_k[:, cols]
        key_squares += key * key
        crossing += scaled[:, cols] * key
    key_squares = jnp.sum(key_squares, axis=1, keepdims=True)
    crossing = jnp.sum(crossing, axis=1, keepdims=True)
    lanes = lax.broadcasted_iota(jnp.int32, (requests, LANES), 1)
    packed = jnp.where(lanes == 0, hidden_squares, jnp.where(lanes == 1, key_squares,
                       jnp.where(lanes == 2, crossing, 0.0)))
    stats[0] = packed.T[:8]
    for m in range(heads - 1, 0, -1):
        there(stats.at[0], stats.at[m], stat_send.at[0], stat_recv.at[0], me_p, me_t ^ m).start()

    multiply(last, wv, acc_v, 0, heads)

    others = there(stats.at[pl.ds(1, heads - 1)], stats.at[pl.ds(1, heads - 1)], stat_send.at[0], stat_recv.at[0],
                   me_p, me_t)
    others.wait_recv()
    summed = stats[0]
    for m in range(1, heads):
        summed += stats[m]
    hidden_total, key_total, cross_total = summed[0:1], summed[1:2], summed[2:3]
    agreement = (cross_total * lax.rsqrt(hidden_total / model + epsilon)
                 * lax.rsqrt(key_total / model + epsilon))
    gate = jax.nn.sigmoid(agreement / math.sqrt(model))
    gate = jnp.broadcast_to(gate, (LANES, requests)).T
    for c in range(columns // LANES):
        cols = slice(c * LANES, (c + 1) * LANES)
        out_ref[:, cols] = (hidden[:, cols].astype(F32) + gate * acc_v[:, cols]).astype(BF16)

    some = pl.ds(0, owners - 1)
    there(lists_out.at[some], lists_in.at[some], list_send.at[0], list_recv.at[0], me_p, me_t).wait_send()
    there(sending.at[some], rows.at[some], row_send.at[0], row_recv.at[0], me_p, me_t).wait_send()
    few = pl.ds(0, heads - 1)
    there(mem.at[few], mem.at[few], pass_send.at[0], pass_recv.at[0], me_p, me_t).wait_send()
    others.wait_send()


def local(groups, heads, hidden, hash_rows, memory_table, key_weight, value_weight, hidden_gain, key_gain):
    requests, columns = hidden.shape
    held, width = memory_table.shape
    owners = groups * heads
    assert hash_rows.shape[1] == 1 and heads & (heads - 1) == 0 and heads > 1
    assert groups & (groups - 1) == 0 and requests == LANES
    slots = max(8, 2 * max(1, hash_rows.size // owners))
    sizes = []
    left = width - LANES
    while left > 0:
        sizes.append(min(2 * LANES, left))
        left -= sizes[-1]
    sizes.append(LANES)
    any_space = pl.BlockSpec(memory_space=pl.ANY)
    vmem = pl.BlockSpec(memory_space=pltpu.VMEM)
    dma = pltpu.SemaphoreType.DMA
    return pl.pallas_call(
        functools.partial(kernel, groups, heads, slots, tuple(sizes)),
        out_shape=jax.ShapeDtypeStruct((requests, columns), BF16),
        in_specs=[any_space] * 7,
        out_specs=vmem,
        scratch_shapes=[
            pltpu.VMEM((1, 1, requests), jnp.int32),
            pltpu.VMEM((columns,), F32),
            pltpu.VMEM((columns,), F32),
            pltpu.VMEM((held, width), BF16),
            pltpu.VMEM((requests, columns), BF16),
            pltpu.VMEM((requests, columns), F32),
            pltpu.VMEM((heads * width, columns), BF16),
            pltpu.VMEM((heads * width, columns), BF16),
            pltpu.VMEM((owners, 1, LANES), F32),
            pltpu.VMEM((owners, 1, LANES), F32),
            pltpu.VMEM((owners, slots, width), BF16),
            pltpu.VMEM((owners, slots, width), BF16),
            pltpu.VMEM((requests, owners * slots), BF16),
            pltpu.VMEM((heads, width // LANES, requests, LANES), BF16),
            pltpu.VMEM((requests, columns), F32),
            pltpu.VMEM((requests, columns), F32),
            pltpu.VMEM((heads, 8, requests), F32),
            dma((7,)), dma((1,)), dma((1,)), dma((1,)), dma((len(sizes),)),
            dma((1,)), dma((len(sizes) * (heads - 1),)), dma((1,)), dma((1,)),
        ],
        compiler_params=pltpu.CompilerParams(
            collective_id=0, has_side_effects=True, vmem_limit_bytes=60 * 1024 * 1024),
    )(hash_rows.reshape(1, 1, requests), hidden_gain, key_gain,
      memory_table, hidden, key_weight, value_weight)


def solution(mesh):
    return jax.shard_map(
        functools.partial(local, mesh.shape["dp"], mesh.shape["tensor"]),
        mesh=mesh,
        in_specs=(
            P("dp", "tensor"),
            P("dp", "tensor"),
            P(("dp", "tensor"), None),
            P(None, "tensor"),
            P(None, "tensor"),
            P("tensor"),
            P("tensor"),
        ),
        out_specs=P("dp", "tensor"),
        check_vma=False,
    )
```

```python
import functools
import math

import jax
import jax.numpy as jnp
from jax import lax
from jax.experimental import pallas as pl
from jax.experimental.pallas import tpu as pltpu
from jax.sharding import PartitionSpec as P

MESH = pl.DeviceIdType.MESH
epsilon = 1e-06
F32, BF16 = jnp.float32, jnp.bfloat16
LANES = 128


def dot(a, b):
    return jnp.dot(a, b, preferred_element_type=F32)


def kernel(groups, heads, slots, sizes, ids_hbm, hg_hbm, kg_hbm, table_hbm, hidden_hbm, wk_hbm, wv_hbm, out_ref,
           ids, hg, kg, table, hidden, scaled, wk, wv, lists_out, lists_in, sending, rows, place, mem, acc_k, acc_v,
           stats, local_sem, list_send, list_recv, row_send, row_recv, pass_send, pass_recv, stat_send, stat_recv):
    me_p, me_t = lax.axis_index("dp"), lax.axis_index("tensor")
    me = me_p * heads + me_t
    owners = groups * heads
    held, width = table.shape
    requests, columns = hidden.shape
    model = columns * heads
    part = 256 if columns % 256 == 0 else 128
    starts = [sum(sizes[:c]) for c in range(len(sizes))]
    last = len(sizes) - 1

    def here(source, target, sem):
        return pltpu.make_async_copy(source, target, sem)

    def there(source, target, send, recv, p, t):
        return pltpu.make_async_remote_copy(
            src_ref=source, dst_ref=target, send_sem=send, recv_sem=recv,
            device_id={"dp": p, "tensor": t}, device_id_type=MESH)

    def peer(i):
        j = owners - i
        return me_p ^ lax.div(j, heads), me_t ^ lax.rem(j, heads)

    barrier = pltpu.get_barrier_semaphore()

    @pl.loop(1, owners)
    def _(i):
        p, t = peer(i)
        pl.semaphore_signal(barrier, inc=1, device_id={"dp": p, "tensor": t}, device_id_type=MESH)

    ids_copy = here(ids_hbm, ids, local_sem.at[0])
    table_copy = here(table_hbm, table, local_sem.at[1])
    hidden_copy = here(hidden_hbm, hidden, local_sem.at[2])
    hg_copy = here(hg_hbm, hg, local_sem.at[3])
    kg_copy = here(kg_hbm, kg, local_sem.at[4])
    for copy in (ids_copy, table_copy, hidden_copy, hg_copy, kg_copy):
        copy.start()
    for start, size in zip(starts, sizes):
        for k, (source, target) in enumerate(((wk_hbm, wk), (wv_hbm, wv))):
            for h in range(heads):
                here(source.at[pl.ds(h * width + start, size), :],
                     target.at[pl.ds(heads * start + h * size, size), :], local_sem.at[5 + k]).start()

    ids_copy.wait()
    sub = lax.broadcasted_iota(jnp.int32, (requests, requests), 0)
    lane = lax.broadcasted_iota(jnp.int32, (requests, requests), 1)
    numbers = ids[0].astype(F32)
    owner_row = jnp.floor((numbers + 0.5) * (1.0 / held))
    local_row = numbers - owner_row * held
    owner = jnp.broadcast_to(owner_row, (requests, requests))
    column = jnp.sum(jnp.where(sub == lane, owner, 0.0), axis=1, keepdims=True)
    inside = jnp.sum(jnp.where(sub == lane, jnp.broadcast_to(local_row, (requests, requests)), 0.0), axis=1, keepdims=True)
    rank = jnp.sum(jnp.where((owner == column) & (lane < sub), 1.0, 0.0), axis=1, keepdims=True)
    spots = lax.broadcasted_iota(jnp.int32, (requests, owners * slots), 1).astype(F32)
    place[...] = jnp.where(spots == column * slots + rank, 1.0, 0.0).astype(BF16)
    whose = lax.broadcasted_iota(jnp.int32, (owners, requests), 0).astype(F32)
    belongs = jnp.where(whose == owner_row, 1.0, 0.0).astype(BF16)
    slot_lane = lax.broadcasted_iota(jnp.int32, (requests, LANES), 1).astype(F32)
    ranked = jnp.where(slot_lane == rank, inside, 0.0).astype(BF16)
    lists_out[...] = dot(belongs, ranked).reshape(owners, 1, LANES)

    here(lists_out.at[me], lists_in.at[me], list_recv.at[0]).start()
    pl.semaphore_wait(barrier, owners - 1)

    @pl.loop(1, owners)
    def _(i):
        p, t = peer(i)
        there(lists_out.at[p * heads + t], lists_in.at[me], list_send.at[0], list_recv.at[0], p, t).start()

    hidden_copy.wait()
    hg_copy.wait()
    kg_copy.wait()
    hidden_squares = jnp.zeros((requests, LANES), F32)
    for c in range(columns // LANES):
        cols = slice(c * LANES, (c + 1) * LANES)
        value = hidden[:, cols].astype(F32)
        hidden_squares += value * value
        scaled[:, cols] = value * (hg[cols] * kg[cols]).reshape(1, LANES)
    hidden_squares = jnp.sum(hidden_squares, axis=1, keepdims=True)

    table_copy.wait()
    there(lists_out, lists_in, list_send.at[0], list_recv.at[0], me_p, me_t).wait_recv()
    shape = (owners, slots, LANES)
    diagonal = lax.broadcasted_iota(jnp.int32, shape, 1) == lax.broadcasted_iota(jnp.int32, shape, 2)
    wanted = jnp.sum(jnp.where(diagonal, jnp.broadcast_to(lists_in[...], shape), 0.0), axis=2, keepdims=True)
    wanted = wanted.reshape(owners * slots, 1)
    choose = jnp.where(
        lax.broadcasted_iota(jnp.int32, (owners * slots, held), 1).astype(F32) == wanted, 1.0, 0.0).astype(BF16)

    for c, (start, size) in enumerate(zip(starts, sizes)):
        cols = pl.ds(start, size)
        block = dot(choose, table[:, cols])
        sending[:, :, cols] = block.reshape(owners, slots, size).astype(BF16)
        here(sending.at[me, :, cols], rows.at[me, :, cols], row_recv.at[c]).start()

        @pl.loop(1, owners)
        def _(i):
            p, t = peer(i)
            there(sending.at[p * heads + t, :, cols], rows.at[me, :, cols], row_send.at[0], row_recv.at[c], p, t).start()

    def blocks(c):
        return pl.ds(starts[c] // LANES, sizes[c] // LANES)

    def share(c, h, m):
        return lambda n: there(mem.at[h, blocks(c)], mem.at[h, blocks(c)], pass_send.at[0],
                               pass_recv.at[c * (heads - 1) + n - 1], me_p, me_t ^ m)

    def arrived(c, n):
        return there(mem.at[me_t ^ n, blocks(c)], mem.at[me_t ^ n, blocks(c)], pass_send.at[0],
                     pass_recv.at[c * (heads - 1) + n - 1], me_p, me_t ^ n)

    def relayed(c):
        return c != last

    def compact(c):
        cols = pl.ds(starts[c], sizes[c])
        there(sending.at[:, :, cols], rows.at[:, :, cols], row_send.at[0], row_recv.at[c], me_p, me_t).wait_recv()
        mine = dot(place[...], rows[:, :, cols].reshape(owners * slots, sizes[c])).astype(BF16)
        for b in range(sizes[c] // LANES):
            mem[me_t, starts[c] // LANES + b] = mine[:, b * LANES:(b + 1) * LANES]
        for m in list(range(2, heads)) + [1]:
            if m % 2 == 0 or m == 1 or not relayed(c):
                share(c, me_t, m)(m).start()

    def relay(c):
        if relayed(c):
            for m in range(2, heads, 2):
                arrived(c, m).wait_recv()
                share(c, me_t ^ m, 1)(m | 1).start()

    def operand(c, base, count):
        b0, nb = starts[c] // LANES, sizes[c] // LANES
        return jnp.concatenate([mem[base + h, b0 + b] for h in range(count) for b in range(nb)], axis=1)

    def multiply(c, w, acc, base, count):
        x = operand(c, base, count)
        first = heads * starts[c] + base * sizes[c]
        if not isinstance(first, int):
            first = pl.multiple_of(first, LANES)
        depth = pl.ds(first, count * sizes[c])
        for n in range(columns // part):
            cols = pl.ds(n * part, part)
            value = dot(x, w[depth, cols])
            acc[:, cols] = value if c == 0 else acc[:, cols] + value

    def gathered(c):
        for m in range(1, heads):
            if not relayed(c) or m % 2:
                arrived(c, m).wait_recv()

    def product(c):
        gathered(c)
        multiply(c, wk, acc_k, 0, heads)
        multiply(c, wv, acc_v, 0, heads)

    for c in range(last + 1):
        compact(c)
        if c >= 1:
            relay(c - 1)
        if c == 1:
            here(wk_hbm, wk, local_sem.at[5]).wait()
            here(wv_hbm, wv, local_sem.at[6]).wait()
        if c >= 2:
            product(c - 2)
    product(last - 1)

    pair = me_t - lax.rem(me_t, 2)
    arrived(last, 1).wait_recv()
    multiply(last, wk, acc_k, pair, 2)
    for m in range(2, heads, 2):
        arrived(last, m).wait_recv()
        arrived(last, m + 1).wait_recv()
        multiply(last, wk, acc_k, pair ^ m, 2)

    key_squares = jnp.zeros((requests, LANES), F32)
    crossing = jnp.zeros((requests, LANES), F32)
    for c in range(columns // LANES):
        cols = slice(c * LANES, (c + 1) * LANES)
        key = acc_k[:, cols]
        key_squares += key * key
        crossing += scaled[:, cols] * key
    key_squares = jnp.sum(key_squares, axis=1, keepdims=True)
    crossing = jnp.sum(crossing, axis=1, keepdims=True)
    lanes = lax.broadcasted_iota(jnp.int32, (requests, LANES), 1)
    packed = jnp.where(lanes == 0, hidden_squares, jnp.where(lanes == 1, key_squares,
                       jnp.where(lanes == 2, crossing, 0.0)))
    stats[0] = packed.T[:8]
    for m in range(heads - 1, 0, -1):
        there(stats.at[0], stats.at[m], stat_send.at[0], stat_recv.at[0], me_p, me_t ^ m).start()

    multiply(last, wv, acc_v, 0, heads)

    others = there(stats.at[pl.ds(1, heads - 1)], stats.at[pl.ds(1, heads - 1)], stat_send.at[0], stat_recv.at[0],
                   me_p, me_t)
    others.wait_recv()
    summed = stats[0]
    for m in range(1, heads):
        summed += stats[m]
    hidden_total, key_total, cross_total = summed[0:1], summed[1:2], summed[2:3]
    agreement = (cross_total * lax.rsqrt(hidden_total / model + epsilon)
                 * lax.rsqrt(key_total / model + epsilon))
    gate = jax.nn.sigmoid(agreement / math.sqrt(model))
    gate = jnp.broadcast_to(gate, (LANES, requests)).T
    for c in range(columns // LANES):
        cols = slice(c * LANES, (c + 1) * LANES)
        out_ref[:, cols] = (hidden[:, cols].astype(F32) + gate * acc_v[:, cols]).astype(BF16)

    some = pl.ds(0, owners - 1)
    there(lists_out.at[some], lists_in.at[some], list_send.at[0], list_recv.at[0], me_p, me_t).wait_send()
    there(sending.at[some], rows.at[some], row_send.at[0], row_recv.at[0], me_p, me_t).wait_send()
    few = pl.ds(0, heads - 1)
    there(mem.at[few], mem.at[few], pass_send.at[0], pass_recv.at[0], me_p, me_t).wait_send()
    others.wait_send()


def local(groups, heads, hidden, hash_rows, memory_table, key_weight, value_weight, hidden_gain, key_gain):
    requests, columns = hidden.shape
    held, width = memory_table.shape
    owners = groups * heads
    assert hash_rows.shape[1] == 1 and heads & (heads - 1) == 0 and heads > 1
    assert groups & (groups - 1) == 0 and requests == LANES
    slots = max(8, 2 * max(1, hash_rows.size // owners))
    sizes = []
    left = width - LANES
    while left > 0:
        sizes.append(min(2 * LANES, left))
        left -= sizes[-1]
    sizes.append(LANES)
    any_space = pl.BlockSpec(memory_space=pl.ANY)
    vmem = pl.BlockSpec(memory_space=pltpu.VMEM)
    dma = pltpu.SemaphoreType.DMA
    return pl.pallas_call(
        functools.partial(kernel, groups, heads, slots, tuple(sizes)),
        out_shape=jax.ShapeDtypeStruct((requests, columns), BF16),
        in_specs=[any_space] * 7,
        out_specs=vmem,
        scratch_shapes=[
            pltpu.VMEM((1, 1, requests), jnp.int32),
            pltpu.VMEM((columns,), F32),
            pltpu.VMEM((columns,), F32),
            pltpu.VMEM((held, width), BF16),
            pltpu.VMEM((requests, columns), BF16),
            pltpu.VMEM((requests, columns), F32),
            pltpu.VMEM((heads * width, columns), BF16),
            pltpu.VMEM((heads * width, columns), BF16),
            pltpu.VMEM((owners, 1, LANES), F32),
            pltpu.VMEM((owners, 1, LANES), F32),
            pltpu.VMEM((owners, slots, width), BF16),
            pltpu.VMEM((owners, slots, width), BF16),
            pltpu.VMEM((requests, owners * slots), BF16),
            pltpu.VMEM((heads, width // LANES, requests, LANES), BF16),
            pltpu.VMEM((requests, columns), F32),
            pltpu.VMEM((requests, columns), F32),
            pltpu.VMEM((heads, 8, requests), F32),
            dma((7,)), dma((1,)), dma((1,)), dma((1,)), dma((len(sizes),)),
            dma((1,)), dma((len(sizes) * (heads - 1),)), dma((1,)), dma((1,)),
        ],
        compiler_params=pltpu.CompilerParams(
            collective_id=0, has_side_effects=True, vmem_limit_bytes=44 * 1024 * 1024),
    )(*(pltpu.with_memory_space_constraint(x, pltpu.HBM) for x in (
        hash_rows.reshape(1, 1, requests), hidden_gain, key_gain, memory_table, hidden, key_weight, value_weight)))


def solution(mesh):
    return jax.shard_map(
        functools.partial(local, mesh.shape["dp"], mesh.shape["tensor"]),
        mesh=mesh,
        in_specs=(
            P("dp", "tensor"),
            P("dp", "tensor"),
            P(("dp", "tensor"), None),
            P(None, "tensor"),
            P(None, "tensor"),
            P("tensor"),
            P("tensor"),
        ),
        out_specs=P("dp", "tensor"),
        check_vma=False,
    )
```

```python
import functools
import math

import jax
import jax.numpy as jnp
from jax import lax
from jax.experimental import pallas as pl
from jax.experimental.pallas import tpu as pltpu
from jax.sharding import PartitionSpec as P

MESH = pl.DeviceIdType.MESH
epsilon = 1e-06
F32, BF16 = jnp.float32, jnp.bfloat16
LANES = 128


def dot(a, b):
    return jnp.dot(a, b, preferred_element_type=F32)


def kernel(groups, heads, slots, sizes, ids_hbm, hg_hbm, kg_hbm, table_hbm, hidden_hbm, wk_hbm, wv_hbm, out_ref,
           ids, hg, kg, table, hidden, scaled, wk, wv, lists_out, lists_in, sending, rows, place, mem, acc_k, acc_v,
           stats, local_sem, list_send, list_recv, row_send, row_recv, pass_send, pass_recv, stat_send, stat_recv,
           lend_send, lend_recv):
    me_p, me_t = lax.axis_index("dp"), lax.axis_index("tensor")
    me = me_p * heads + me_t
    owners = groups * heads
    held, width = table_hbm.shape
    requests, columns = hidden.shape
    model = columns * heads
    part = 256 if columns % 256 == 0 else 128
    starts = [sum(sizes[:c]) for c in range(len(sizes))]
    last = len(sizes) - 1

    def here(source, target, sem):
        return pltpu.make_async_copy(source, target, sem)

    def there(source, target, send, recv, p, t):
        return pltpu.make_async_remote_copy(
            src_ref=source, dst_ref=target, send_sem=send, recv_sem=recv,
            device_id={"dp": p, "tensor": t}, device_id_type=MESH)

    def split(device):
        return lax.div(device, heads), lax.rem(device, heads)

    def peer(i):
        return split(me ^ (owners - i))

    def pairing(device):
        p, t = split(device)
        odd = lax.rem(t, 2)
        middle = lax.rem(lax.div(lax.div(p, groups // 4) + 1, 2), 2)
        even_side = middle * (groups // 2 * heads) + (1 - middle) * heads
        even_way = even_side + middle * (groups // 4 * heads)
        across = heads // 2
        return odd * across + (1 - odd) * even_way, odd * across + (1 - odd) * even_side

    way, side = pairing(me)
    partner = me ^ way

    def other(i):
        j = owners - i
        return me ^ jnp.where(j > way, j, j - 1)

    def server(owner):
        away, bit = pairing(owner)
        away = lax.rem(lax.div(me ^ owner, bit), 2) * away
        return owner ^ away, me ^ away

    barrier = pltpu.get_barrier_semaphore()

    @pl.loop(1, owners)
    def _(i):
        p, t = peer(i)
        pl.semaphore_signal(barrier, inc=1, device_id={"dp": p, "tensor": t}, device_id_type=MESH)

    ids_copy = here(ids_hbm, ids, local_sem.at[0])
    table_copy = here(table_hbm, table.at[pl.ds(0, held)], local_sem.at[1])
    hidden_copy = here(hidden_hbm, hidden, local_sem.at[2])
    hg_copy = here(hg_hbm, hg, local_sem.at[3])
    kg_copy = here(kg_hbm, kg, local_sem.at[4])
    for copy in (ids_copy, table_copy, hidden_copy, hg_copy, kg_copy):
        copy.start()
    for start, size in zip(starts, sizes):
        for k, (source, target) in enumerate(((wk_hbm, wk), (wv_hbm, wv))):
            for h in range(heads):
                here(source.at[pl.ds(h * width + start, size), :],
                     target.at[pl.ds(heads * start + h * size, size), :], local_sem.at[5 + k]).start()

    ids_copy.wait()
    sub = lax.broadcasted_iota(jnp.int32, (requests, requests), 0)
    lane = lax.broadcasted_iota(jnp.int32, (requests, requests), 1)
    numbers = ids[0].astype(F32)
    owner_row = jnp.floor((numbers + 0.5) * (1.0 / held))
    local_row = numbers - owner_row * held
    owner = jnp.broadcast_to(owner_row, (requests, requests))
    column = jnp.sum(jnp.where(sub == lane, owner, 0.0), axis=1, keepdims=True)
    inside = jnp.sum(jnp.where(sub == lane, jnp.broadcast_to(local_row, (requests, requests)), 0.0), axis=1, keepdims=True)
    rank = jnp.sum(jnp.where((owner == column) & (lane < sub), 1.0, 0.0), axis=1, keepdims=True)
    spots = lax.broadcasted_iota(jnp.int32, (requests, owners * slots), 1).astype(F32)
    place[...] = jnp.where(spots == column * slots + rank, 1.0, 0.0).astype(BF16)
    whose = lax.broadcasted_iota(jnp.int32, (owners, requests), 0).astype(F32)
    belongs = jnp.where(whose == owner_row, 1.0, 0.0).astype(BF16)
    slot_lane = lax.broadcasted_iota(jnp.int32, (requests, LANES), 1).astype(F32)
    ranked = jnp.where(slot_lane == rank, inside, 0.0).astype(BF16)
    lists_out[...] = dot(belongs, ranked).reshape(owners, 1, LANES)

    here(lists_out.at[me], lists_in.at[me], list_recv.at[0]).start()
    here(lists_out.at[partner], lists_in.at[partner], list_recv.at[0]).start()
    table_copy.wait()
    pl.semaphore_wait(barrier, owners - 1)

    def lend(c):
        cols = pl.ds(starts[c], sizes[c])
        return there(table.at[pl.ds(0, held), cols], table.at[pl.ds(held, held), cols], lend_send.at[0], lend_recv.at[c],
                     *split(partner))

    lend(0).start()

    @pl.loop(1, owners - 1)
    def _(i):
        owner = other(i)
        target, known = server(owner)
        there(lists_out.at[owner], lists_in.at[known], list_send.at[0], list_recv.at[0], *split(target)).start()

    for c in range(1, len(sizes)):
        lend(c).start()

    hidden_copy.wait()
    hg_copy.wait()
    kg_copy.wait()
    hidden_squares = jnp.zeros((requests, LANES), F32)
    for c in range(columns // LANES):
        cols = slice(c * LANES, (c + 1) * LANES)
        value = hidden[:, cols].astype(F32)
        hidden_squares += value * value
        scaled[:, cols] = value * (hg[cols] * kg[cols]).reshape(1, LANES)
    hidden_squares = jnp.sum(hidden_squares, axis=1, keepdims=True)

    there(lists_out, lists_in, list_send.at[0], list_recv.at[0], me_p, me_t).wait_recv()
    shape = (owners, slots, LANES)
    diagonal = lax.broadcasted_iota(jnp.int32, shape, 1) == lax.broadcasted_iota(jnp.int32, shape, 2)
    wanted = jnp.sum(jnp.where(diagonal, jnp.broadcast_to(lists_in[...], shape), 0.0), axis=2, keepdims=True)
    wanted = wanted.reshape(owners * slots, 1)
    whom = lax.broadcasted_iota(jnp.int32, (owners * slots, 1), 0) // slots
    wanted = wanted + jnp.where(((whom ^ me) & side) != 0, float(held), 0.0)
    choose = jnp.where(
        lax.broadcasted_iota(jnp.int32, (owners * slots, 2 * held), 1).astype(F32) == wanted, 1.0, 0.0).astype(BF16)

    for c, (start, size) in enumerate(zip(starts, sizes)):
        cols = pl.ds(start, size)
        lend(c).wait_recv()
        block = dot(choose, table[:, cols])
        sending[:, :, cols] = block.reshape(owners, slots, size).astype(BF16)
        for owner in (me, partner):
            here(sending.at[owner, :, cols], rows.at[owner, :, cols], row_recv.at[c]).start()

        @pl.loop(1, owners - 1)
        def _(i):
            place_of = other(i)
            away = lax.rem(lax.div(me ^ place_of, side), 2) * way
            there(sending.at[place_of, :, cols], rows.at[me ^ away, :, cols], row_send.at[0], row_recv.at[c],
                  *split(place_of ^ away)).start()

    def blocks(c):
        return pl.ds(starts[c] // LANES, sizes[c] // LANES)

    def share(c, h, m):
        return lambda n: there(mem.at[h, blocks(c)], mem.at[h, blocks(c)], pass_send.at[0],
                               pass_recv.at[c * (heads - 1) + n - 1], me_p, me_t ^ m)

    def arrived(c, n):
        return there(mem.at[me_t ^ n, blocks(c)], mem.at[me_t ^ n, blocks(c)], pass_send.at[0],
                     pass_recv.at[c * (heads - 1) + n - 1], me_p, me_t ^ n)

    def relayed(c):
        return c != last

    def compact(c):
        cols = pl.ds(starts[c], sizes[c])
        there(sending.at[:, :, cols], rows.at[:, :, cols], row_send.at[0], row_recv.at[c], me_p, me_t).wait_recv()
        mine = dot(place[...], rows[:, :, cols].reshape(owners * slots, sizes[c])).astype(BF16)
        for b in range(sizes[c] // LANES):
            mem[me_t, starts[c] // LANES + b] = mine[:, b * LANES:(b + 1) * LANES]
        for m in list(range(2, heads)) + [1]:
            if m % 2 == 0 or m == 1 or not relayed(c):
                share(c, me_t, m)(m).start()

    def relay(c):
        if relayed(c):
            for m in range(2, heads, 2):
                arrived(c, m).wait_recv()
                share(c, me_t ^ m, 1)(m | 1).start()

    def operand(c, base, count):
        b0, nb = starts[c] // LANES, sizes[c] // LANES
        return jnp.concatenate([mem[base + h, b0 + b] for h in range(count) for b in range(nb)], axis=1)

    def multiply(c, w, acc, base, count):
        x = operand(c, base, count)
        first = heads * starts[c] + base * sizes[c]
        if not isinstance(first, int):
            first = pl.multiple_of(first, LANES)
        depth = pl.ds(first, count * sizes[c])
        for n in range(columns // part):
            cols = pl.ds(n * part, part)
            value = dot(x, w[depth, cols])
            acc[:, cols] = value if c == 0 else acc[:, cols] + value

    def gathered(c):
        for m in range(1, heads):
            if not relayed(c) or m % 2:
                arrived(c, m).wait_recv()

    def product(c):
        gathered(c)
        multiply(c, wk, acc_k, 0, heads)
        multiply(c, wv, acc_v, 0, heads)

    for c in range(last + 1):
        compact(c)
        if c >= 1:
            relay(c - 1)
        if c == 1:
            here(wk_hbm, wk, local_sem.at[5]).wait()
            here(wv_hbm, wv, local_sem.at[6]).wait()
        if c >= 2:
            product(c - 2)
    product(last - 1)

    pair = me_t - lax.rem(me_t, 2)
    arrived(last, 1).wait_recv()
    multiply(last, wk, acc_k, pair, 2)
    for m in range(2, heads, 2):
        arrived(last, m).wait_recv()
        arrived(last, m + 1).wait_recv()
        multiply(last, wk, acc_k, pair ^ m, 2)

    key_squares = jnp.zeros((requests, LANES), F32)
    crossing = jnp.zeros((requests, LANES), F32)
    for c in range(columns // LANES):
        cols = slice(c * LANES, (c + 1) * LANES)
        key = acc_k[:, cols]
        key_squares += key * key
        crossing += scaled[:, cols] * key
    key_squares = jnp.sum(key_squares, axis=1, keepdims=True)
    crossing = jnp.sum(crossing, axis=1, keepdims=True)
    lanes = lax.broadcasted_iota(jnp.int32, (requests, LANES), 1)
    packed = jnp.where(lanes == 0, hidden_squares, jnp.where(lanes == 1, key_squares,
                       jnp.where(lanes == 2, crossing, 0.0)))
    stats[0] = packed.T[:8]
    for m in range(heads - 1, 0, -1):
        there(stats.at[0], stats.at[m], stat_send.at[0], stat_recv.at[0], me_p, me_t ^ m).start()

    multiply(last, wv, acc_v, 0, heads)

    others = there(stats.at[pl.ds(1, heads - 1)], stats.at[pl.ds(1, heads - 1)], stat_send.at[0], stat_recv.at[0],
                   me_p, me_t)
    others.wait_recv()
    summed = stats[0]
    for m in range(1, heads):
        summed += stats[m]
    hidden_total, key_total, cross_total = summed[0:1], summed[1:2], summed[2:3]
    agreement = (cross_total * lax.rsqrt(hidden_total / model + epsilon)
                 * lax.rsqrt(key_total / model + epsilon))
    gate = jax.nn.sigmoid(agreement / math.sqrt(model))
    gate = jnp.broadcast_to(gate, (LANES, requests)).T
    for c in range(columns // LANES):
        cols = slice(c * LANES, (c + 1) * LANES)
        out_ref[:, cols] = (hidden[:, cols].astype(F32) + gate * acc_v[:, cols]).astype(BF16)

    some = pl.ds(0, owners - 2)
    there(lists_out.at[some], lists_in.at[some], list_send.at[0], list_recv.at[0], me_p, me_t).wait_send()
    there(sending.at[some], rows.at[some], row_send.at[0], row_recv.at[0], me_p, me_t).wait_send()
    there(table.at[pl.ds(0, held)], table.at[pl.ds(held, held)], lend_send.at[0], lend_recv.at[0], me_p, me_t).wait_send()
    few = pl.ds(0, heads - 1)
    there(mem.at[few], mem.at[few], pass_send.at[0], pass_recv.at[0], me_p, me_t).wait_send()
    others.wait_send()


def local(groups, heads, hidden, hash_rows, memory_table, key_weight, value_weight, hidden_gain, key_gain):
    requests, columns = hidden.shape
    held, width = memory_table.shape
    owners = groups * heads
    assert hash_rows.shape[1] == 1 and heads & (heads - 1) == 0 and heads > 1
    assert groups & (groups - 1) == 0 and requests == LANES and groups >= 4 and heads >= 4
    slots = max(8, 2 * max(1, hash_rows.size // owners))
    sizes = []
    left = width - LANES
    while left > 0:
        sizes.append(min(2 * LANES, left))
        left -= sizes[-1]
    sizes.append(LANES)
    any_space = pl.BlockSpec(memory_space=pl.ANY)
    vmem = pl.BlockSpec(memory_space=pltpu.VMEM)
    dma = pltpu.SemaphoreType.DMA
    return pl.pallas_call(
        functools.partial(kernel, groups, heads, slots, tuple(sizes)),
        out_shape=jax.ShapeDtypeStruct((requests, columns), BF16),
        in_specs=[any_space] * 7,
        out_specs=vmem,
        scratch_shapes=[
            pltpu.VMEM((1, 1, requests), jnp.int32),
            pltpu.VMEM((columns,), F32),
            pltpu.VMEM((columns,), F32),
            pltpu.VMEM((2 * held, width), BF16),
            pltpu.VMEM((requests, columns), BF16),
            pltpu.VMEM((requests, columns), F32),
            pltpu.VMEM((heads * width, columns), BF16),
            pltpu.VMEM((heads * width, columns), BF16),
            pltpu.VMEM((owners, 1, LANES), F32),
            pltpu.VMEM((owners, 1, LANES), F32),
            pltpu.VMEM((owners, slots, width), BF16),
            pltpu.VMEM((owners, slots, width), BF16),
            pltpu.VMEM((requests, owners * slots), BF16),
            pltpu.VMEM((heads, width // LANES, requests, LANES), BF16),
            pltpu.VMEM((requests, columns), F32),
            pltpu.VMEM((requests, columns), F32),
            pltpu.VMEM((heads, 8, requests), F32),
            dma((7,)), dma((1,)), dma((1,)), dma((1,)), dma((len(sizes),)),
            dma((1,)), dma((len(sizes) * (heads - 1),)), dma((1,)), dma((1,)),
            dma((1,)), dma((len(sizes),)),
        ],
        compiler_params=pltpu.CompilerParams(
            collective_id=0, has_side_effects=True, vmem_limit_bytes=44 * 1024 * 1024),
    )(*(pltpu.with_memory_space_constraint(x, pltpu.HBM) for x in (
        hash_rows.reshape(1, 1, requests), hidden_gain, key_gain, memory_table, hidden, key_weight, value_weight)))


def solution(mesh):
    return jax.shard_map(
        functools.partial(local, mesh.shape["dp"], mesh.shape["tensor"]),
        mesh=mesh,
        in_specs=(
            P("dp", "tensor"),
            P("dp", "tensor"),
            P(("dp", "tensor"), None),
            P(None, "tensor"),
            P(None, "tensor"),
            P("tensor"),
            P("tensor"),
        ),
        out_specs=P("dp", "tensor"),
        check_vma=False,
    )
```

```python
import functools
import math

import jax
import jax.numpy as jnp
from jax import lax
from jax.experimental import pallas as pl
from jax.experimental.pallas import tpu as pltpu
from jax.sharding import PartitionSpec as P

MESH = pl.DeviceIdType.MESH
epsilon = 1e-06
F32, BF16 = jnp.float32, jnp.bfloat16
LANES = 128


def dot(a, b):
    return jnp.dot(a, b, preferred_element_type=F32)


def kernel(groups, heads, slots, sizes, ids_hbm, hg_hbm, kg_hbm, table_hbm, hidden_hbm, wk_hbm, wv_hbm, out_ref,
           ids, hg, kg, table, hidden, scaled, wk, wv, lists_out, lists_in, sending, rows, place, mem, acc_k, acc_v,
           stats, local_sem, list_send, list_recv, row_send, row_recv, pass_send, pass_recv, stat_send, stat_recv,
           lend_send, lend_recv):
    me_p, me_t = lax.axis_index("dp"), lax.axis_index("tensor")
    me = me_p * heads + me_t
    owners = groups * heads
    held, width = table_hbm.shape
    requests, columns = hidden.shape
    model = columns * heads
    part = 256 if columns % 256 == 0 else 128
    starts = [sum(sizes[:c]) for c in range(len(sizes))]
    last = len(sizes) - 1

    def here(source, target, sem):
        return pltpu.make_async_copy(source, target, sem)

    def there(source, target, send, recv, p, t):
        return pltpu.make_async_remote_copy(
            src_ref=source, dst_ref=target, send_sem=send, recv_sem=recv,
            device_id={"dp": p, "tensor": t}, device_id_type=MESH)

    head_bits = heads.bit_length() - 1

    def split(device):
        return device >> head_bits, device & (heads - 1)

    def peer(i):
        return split(me ^ (owners - i))

    across, low, high, quarter = heads // 2, heads, owners // 2, owners // 4

    def pairing(device):
        even = (device & 1) == 0
        middle = ((device + quarter) & high) != 0
        return (jnp.where(even, across, jnp.where(middle, high + quarter, low)),
                jnp.where(even, across, jnp.where(middle, high, low)))

    way, side = pairing(me)
    partner = me ^ way

    def other(i):
        j = owners - i
        return me ^ jnp.where(j > way, j, j - 1)

    def server(owner):
        away, bit = pairing(owner)
        away = jnp.where(((me ^ owner) & bit) != 0, away, 0)
        return owner ^ away, me ^ away

    barrier = pltpu.get_barrier_semaphore()

    ids_copy = here(ids_hbm, ids, local_sem.at[0])
    table_copy = here(table_hbm, table.at[pl.ds(0, held)], local_sem.at[1])
    hidden_copy = here(hidden_hbm, hidden, local_sem.at[2])
    hg_copy = here(hg_hbm, hg, local_sem.at[3])
    kg_copy = here(kg_hbm, kg, local_sem.at[4])
    ids_copy.start()
    table_copy.start()

    @pl.loop(1, owners, unroll=owners - 1)
    def _(i):
        p, t = peer(i)
        pl.semaphore_signal(barrier, inc=1, device_id={"dp": p, "tensor": t}, device_id_type=MESH)


    ids_copy.wait()
    sub = lax.broadcasted_iota(jnp.int32, (requests, requests), 0)
    lane = lax.broadcasted_iota(jnp.int32, (requests, requests), 1)
    numbers = ids[0].astype(F32)
    owner_row = jnp.floor((numbers + 0.5) * (1.0 / held))
    local_row = numbers - owner_row * held
    owner = jnp.broadcast_to(owner_row, (requests, requests))
    column = jnp.sum(jnp.where(sub == lane, owner, 0.0), axis=1, keepdims=True)
    inside = jnp.sum(jnp.where(sub == lane, jnp.broadcast_to(local_row, (requests, requests)), 0.0), axis=1, keepdims=True)
    rank = jnp.sum(jnp.where((owner == column) & (lane < sub), 1.0, 0.0), axis=1, keepdims=True)
    spots = lax.broadcasted_iota(jnp.int32, (requests, owners * slots), 1).astype(F32)
    place[...] = jnp.where(spots == column * slots + rank, 1.0, 0.0).astype(BF16)
    whose = lax.broadcasted_iota(jnp.int32, (owners, requests), 0).astype(F32)
    belongs = jnp.where(whose == owner_row, 1.0, 0.0).astype(BF16)
    slot_lane = lax.broadcasted_iota(jnp.int32, (requests, LANES), 1).astype(F32)
    ranked = jnp.where(slot_lane == rank, inside, 0.0).astype(BF16)
    lists_out[...] = dot(belongs, ranked).reshape(owners, 1, LANES)

    here(lists_out.at[me], lists_in.at[me], list_recv.at[0]).start()
    here(lists_out.at[partner], lists_in.at[partner], list_recv.at[0]).start()
    table_copy.wait()
    pl.semaphore_wait(barrier, owners - 1)

    def lend(c):
        cols = pl.ds(starts[c], sizes[c])
        return there(table.at[pl.ds(0, held), cols], table.at[pl.ds(held, held), cols], lend_send.at[0], lend_recv.at[c],
                     *split(partner))

    lend(0).start()

    @pl.loop(1, owners - 1, unroll=5)
    def _(i):
        owner = other(i)
        target, known = server(owner)
        there(lists_out.at[owner], lists_in.at[known], list_send.at[0], list_recv.at[0], *split(target)).start()

    for c in range(1, len(sizes)):
        lend(c).start()
    for copy in (hidden_copy, hg_copy, kg_copy):
        copy.start()
    for start, size in zip(starts, sizes):
        for k, (source, target) in enumerate(((wk_hbm, wk), (wv_hbm, wv))):
            for h in range(heads):
                here(source.at[pl.ds(h * width + start, size), :],
                     target.at[pl.ds(heads * start + h * size, size), :], local_sem.at[5 + k]).start()

    hidden_copy.wait()
    hg_copy.wait()
    kg_copy.wait()
    hidden_squares = jnp.zeros((requests, LANES), F32)
    for c in range(columns // LANES):
        cols = slice(c * LANES, (c + 1) * LANES)
        value = hidden[:, cols].astype(F32)
        hidden_squares += value * value
        scaled[:, cols] = value * (hg[cols] * kg[cols]).reshape(1, LANES)
    hidden_squares = jnp.sum(hidden_squares, axis=1, keepdims=True)

    there(lists_out, lists_in, list_send.at[0], list_recv.at[0], me_p, me_t).wait_recv()
    shape = (owners, slots, LANES)
    diagonal = lax.broadcasted_iota(jnp.int32, shape, 1) == lax.broadcasted_iota(jnp.int32, shape, 2)
    wanted = jnp.sum(jnp.where(diagonal, jnp.broadcast_to(lists_in[...], shape), 0.0), axis=2, keepdims=True)
    wanted = wanted.reshape(owners * slots, 1)
    whom = lax.broadcasted_iota(jnp.int32, (owners * slots, 1), 0) // slots
    wanted = wanted + jnp.where(((whom ^ me) & side) != 0, float(held), 0.0)
    choose = jnp.where(
        lax.broadcasted_iota(jnp.int32, (owners * slots, 2 * held), 1).astype(F32) == wanted, 1.0, 0.0).astype(BF16)

    for c, (start, size) in enumerate(zip(starts, sizes)):
        cols = pl.ds(start, size)
        lend(c).wait_recv()
        block = dot(choose, table[:, cols])
        sending[:, :, cols] = block.reshape(owners, slots, size).astype(BF16)
        for owner in (me, partner):
            here(sending.at[owner, :, cols], rows.at[owner, :, cols], row_recv.at[c]).start()

        @pl.loop(1, owners - 1, unroll=5)
        def _(i):
            place_of = other(1 + lax.rem(i + owners // 2 - 1, owners - 2))
            away = jnp.where(((me ^ place_of) & side) != 0, way, 0)
            there(sending.at[place_of, :, cols], rows.at[me ^ away, :, cols], row_send.at[0], row_recv.at[c],
                  *split(place_of ^ away)).start()

    def blocks(c):
        return pl.ds(starts[c] // LANES, sizes[c] // LANES)

    def share(c, h, m):
        return lambda n: there(mem.at[h, blocks(c)], mem.at[h, blocks(c)], pass_send.at[0],
                               pass_recv.at[c * (heads - 1) + n - 1], me_p, me_t ^ m)

    def arrived(c, n):
        return there(mem.at[me_t ^ n, blocks(c)], mem.at[me_t ^ n, blocks(c)], pass_send.at[0],
                     pass_recv.at[c * (heads - 1) + n - 1], me_p, me_t ^ n)

    def relayed(c):
        return c != last

    def compact(c):
        cols = pl.ds(starts[c], sizes[c])
        there(sending.at[:, :, cols], rows.at[:, :, cols], row_send.at[0], row_recv.at[c], me_p, me_t).wait_recv()
        mine = dot(place[...], rows[:, :, cols].reshape(owners * slots, sizes[c])).astype(BF16)
        for b in range(sizes[c] // LANES):
            mem[me_t, starts[c] // LANES + b] = mine[:, b * LANES:(b + 1) * LANES]
        for m in list(range(2, heads)) + [1]:
            if m % 2 == 0 or m == 1 or not relayed(c):
                share(c, me_t, m)(m).start()

    def relay(c):
        if relayed(c):
            for m in range(2, heads, 2):
                arrived(c, m).wait_recv()
                share(c, me_t ^ m, 1)(m | 1).start()

    def operand(c, base, count):
        b0, nb = starts[c] // LANES, sizes[c] // LANES
        return jnp.concatenate([mem[base + h, b0 + b] for h in range(count) for b in range(nb)], axis=1)

    def multiply(c, w, acc, base, count):
        x = operand(c, base, count)
        first = heads * starts[c] + base * sizes[c]
        if not isinstance(first, int):
            first = pl.multiple_of(first, LANES)
        depth = pl.ds(first, count * sizes[c])
        for n in range(columns // part):
            cols = pl.ds(n * part, part)
            value = dot(x, w[depth, cols])
            acc[:, cols] = value if c == 0 else acc[:, cols] + value

    def gathered(c):
        for m in range(1, heads):
            if not relayed(c) or m % 2:
                arrived(c, m).wait_recv()

    def product(c):
        gathered(c)
        multiply(c, wk, acc_k, 0, heads)
        multiply(c, wv, acc_v, 0, heads)

    for c in range(last + 1):
        compact(c)
        if c >= 1:
            relay(c - 1)
        if c == 1:
            here(wk_hbm, wk, local_sem.at[5]).wait()
            here(wv_hbm, wv, local_sem.at[6]).wait()
        if c >= 2:
            product(c - 2)
    product(last - 1)

    pair = me_t - lax.rem(me_t, 2)
    arrived(last, 1).wait_recv()
    multiply(last, wk, acc_k, pair, 2)
    for m in range(2, heads, 2):
        arrived(last, m).wait_recv()
        arrived(last, m + 1).wait_recv()
        multiply(last, wk, acc_k, pair ^ m, 2)

    key_squares = jnp.zeros((requests, LANES), F32)
    crossing = jnp.zeros((requests, LANES), F32)
    for c in range(columns // LANES):
        cols = slice(c * LANES, (c + 1) * LANES)
        key = acc_k[:, cols]
        key_squares += key * key
        crossing += scaled[:, cols] * key
    key_squares = jnp.sum(key_squares, axis=1, keepdims=True)
    crossing = jnp.sum(crossing, axis=1, keepdims=True)
    lanes = lax.broadcasted_iota(jnp.int32, (requests, LANES), 1)
    packed = jnp.where(lanes == 0, hidden_squares, jnp.where(lanes == 1, key_squares,
                       jnp.where(lanes == 2, crossing, 0.0)))
    stats[0] = packed.T[:8]
    for m in range(heads - 1, 0, -1):
        there(stats.at[0], stats.at[m], stat_send.at[0], stat_recv.at[0], me_p, me_t ^ m).start()

    multiply(last, wv, acc_v, 0, heads)

    others = there(stats.at[pl.ds(1, heads - 1)], stats.at[pl.ds(1, heads - 1)], stat_send.at[0], stat_recv.at[0],
                   me_p, me_t)
    others.wait_recv()
    summed = stats[0]
    for m in range(1, heads):
        summed += stats[m]
    hidden_total, key_total, cross_total = summed[0:1], summed[1:2], summed[2:3]
    agreement = (cross_total * lax.rsqrt(hidden_total / model + epsilon)
                 * lax.rsqrt(key_total / model + epsilon))
    gate = jax.nn.sigmoid(agreement / math.sqrt(model))
    gate = jnp.broadcast_to(gate, (LANES, requests)).T
    for c in range(columns // LANES):
        cols = slice(c * LANES, (c + 1) * LANES)
        out_ref[:, cols] = (hidden[:, cols].astype(F32) + gate * acc_v[:, cols]).astype(BF16)

    some = pl.ds(0, owners - 2)
    there(lists_out.at[some], lists_in.at[some], list_send.at[0], list_recv.at[0], me_p, me_t).wait_send()
    there(sending.at[some], rows.at[some], row_send.at[0], row_recv.at[0], me_p, me_t).wait_send()
    there(table.at[pl.ds(0, held)], table.at[pl.ds(held, held)], lend_send.at[0], lend_recv.at[0], me_p, me_t).wait_send()
    few = pl.ds(0, heads - 1)
    there(mem.at[few], mem.at[few], pass_send.at[0], pass_recv.at[0], me_p, me_t).wait_send()
    others.wait_send()


def local(groups, heads, hidden, hash_rows, memory_table, key_weight, value_weight, hidden_gain, key_gain):
    requests, columns = hidden.shape
    held, width = memory_table.shape
    owners = groups * heads
    assert hash_rows.shape[1] == 1 and heads & (heads - 1) == 0 and heads > 1
    assert groups & (groups - 1) == 0 and requests == LANES and groups >= 4 and heads >= 4
    slots = max(8, 2 * max(1, hash_rows.size // owners))
    sizes = []
    left = width - LANES
    while left > 0:
        sizes.append(min(2 * LANES, left))
        left -= sizes[-1]
    sizes.append(LANES)
    any_space = pl.BlockSpec(memory_space=pl.ANY)
    vmem = pl.BlockSpec(memory_space=pltpu.VMEM)
    dma = pltpu.SemaphoreType.DMA
    return pl.pallas_call(
        functools.partial(kernel, groups, heads, slots, tuple(sizes)),
        out_shape=jax.ShapeDtypeStruct((requests, columns), BF16),
        in_specs=[any_space] * 7,
        out_specs=vmem,
        scratch_shapes=[
            pltpu.VMEM((1, 1, requests), jnp.int32),
            pltpu.VMEM((columns,), F32),
            pltpu.VMEM((columns,), F32),
            pltpu.VMEM((2 * held, width), BF16),
            pltpu.VMEM((requests, columns), BF16),
            pltpu.VMEM((requests, columns), F32),
            pltpu.VMEM((heads * width, columns), BF16),
            pltpu.VMEM((heads * width, columns), BF16),
            pltpu.VMEM((owners, 1, LANES), F32),
            pltpu.VMEM((owners, 1, LANES), F32),
            pltpu.VMEM((owners, slots, width), BF16),
            pltpu.VMEM((owners, slots, width), BF16),
            pltpu.VMEM((requests, owners * slots), BF16),
            pltpu.VMEM((heads, width // LANES, requests, LANES), BF16),
            pltpu.VMEM((requests, columns), F32),
            pltpu.VMEM((requests, columns), F32),
            pltpu.VMEM((heads, 8, requests), F32),
            dma((7,)), dma((1,)), dma((1,)), dma((1,)), dma((len(sizes),)),
            dma((1,)), dma((len(sizes) * (heads - 1),)), dma((1,)), dma((1,)),
            dma((1,)), dma((len(sizes),)),
        ],
        compiler_params=pltpu.CompilerParams(
            collective_id=0, has_side_effects=True, vmem_limit_bytes=44 * 1024 * 1024),
    )(*(pltpu.with_memory_space_constraint(x, pltpu.HBM) for x in (
        hash_rows.reshape(1, 1, requests), hidden_gain, key_gain, memory_table, hidden, key_weight, value_weight)))


def solution(mesh):
    return jax.shard_map(
        functools.partial(local, mesh.shape["dp"], mesh.shape["tensor"]),
        mesh=mesh,
        in_specs=(
            P("dp", "tensor"),
            P("dp", "tensor"),
            P(("dp", "tensor"), None),
            P(None, "tensor"),
            P(None, "tensor"),
            P("tensor"),
            P("tensor"),
        ),
        out_specs=P("dp", "tensor"),
        check_vma=False,
    )
```

```python
import functools
import math

import jax
import jax.numpy as jnp
from jax import lax
from jax.experimental import pallas as pl
from jax.experimental.pallas import tpu as pltpu
from jax.sharding import PartitionSpec as P

MESH = pl.DeviceIdType.MESH
epsilon = 1e-06
F32, BF16 = jnp.float32, jnp.bfloat16
LANES = 128


def dot(a, b):
    return jnp.dot(a, b, preferred_element_type=F32)


def kernel(groups, heads, slots, sizes, ids_hbm, hg_hbm, kg_hbm, table_hbm, hidden_hbm, wk_hbm, wv_hbm, out_ref,
           ids, hg, kg, table, hidden, scaled, wk, wv, lists_out, lists_in, sending, rows, place, mem, acc_k, acc_v,
           stats, local_sem, list_send, list_recv, row_send, row_recv, pass_send, pass_recv, stat_send, stat_recv,
           lend_send, lend_recv):
    me_p, me_t = lax.axis_index("dp"), lax.axis_index("tensor")
    me = me_p * heads + me_t
    owners = groups * heads
    held, width = table_hbm.shape
    requests, columns = hidden.shape
    model = columns * heads
    part = 256 if columns % 256 == 0 else 128
    starts = [sum(sizes[:c]) for c in range(len(sizes))]
    last = len(sizes) - 1

    def here(source, target, sem):
        return pltpu.make_async_copy(source, target, sem)

    def there(source, target, send, recv, p, t):
        return pltpu.make_async_remote_copy(
            src_ref=source, dst_ref=target, send_sem=send, recv_sem=recv,
            device_id={"dp": p, "tensor": t}, device_id_type=MESH)

    head_bits = heads.bit_length() - 1

    def split(device):
        return device >> head_bits, device & (heads - 1)

    def peer(i):
        return split(me ^ (owners - i))

    across, low, high, quarter = heads // 2, heads, owners // 2, owners // 4

    def pairing(device):
        even = (device & 1) == 0
        middle = ((device + quarter) & high) != 0
        return (jnp.where(even, across, jnp.where(middle, high + quarter, low)),
                jnp.where(even, across, jnp.where(middle, high, low)))

    way, side = pairing(me)
    partner = me ^ way

    def other(i):
        j = owners - i
        return me ^ jnp.where(j > way, j, j - 1)

    def server(owner):
        away, bit = pairing(owner)
        away = jnp.where(((me ^ owner) & bit) != 0, away, 0)
        return owner ^ away, me ^ away

    barrier = pltpu.get_barrier_semaphore()

    ids_copy = here(ids_hbm, ids, local_sem.at[0])
    table_copy = here(table_hbm, table.at[pl.ds(0, held)], local_sem.at[1])
    hidden_copy = here(hidden_hbm, hidden, local_sem.at[2])
    hg_copy = here(hg_hbm, hg, local_sem.at[3])
    kg_copy = here(kg_hbm, kg, local_sem.at[4])
    ids_copy.start()
    table_copy.start()

    @pl.loop(1, owners, unroll=owners - 1)
    def _(i):
        p, t = peer(i)
        pl.semaphore_signal(barrier, inc=1, device_id={"dp": p, "tensor": t}, device_id_type=MESH)


    ids_copy.wait()
    sub = lax.broadcasted_iota(jnp.int32, (requests, requests), 0)
    lane = lax.broadcasted_iota(jnp.int32, (requests, requests), 1)
    numbers = ids[0].astype(F32)
    owner_row = jnp.floor((numbers + 0.5) * (1.0 / held))
    local_row = numbers - owner_row * held
    owner = jnp.broadcast_to(owner_row, (requests, requests))
    column = jnp.sum(jnp.where(sub == lane, owner, 0.0), axis=1, keepdims=True)
    inside = jnp.sum(jnp.where(sub == lane, jnp.broadcast_to(local_row, (requests, requests)), 0.0), axis=1, keepdims=True)
    rank = jnp.sum(jnp.where((owner == column) & (lane < sub), 1.0, 0.0), axis=1, keepdims=True)
    spots = lax.broadcasted_iota(jnp.int32, (requests, owners * slots), 1).astype(F32)
    place[...] = jnp.where(spots == column * slots + rank, 1.0, 0.0).astype(BF16)
    whose = lax.broadcasted_iota(jnp.int32, (owners, requests), 0).astype(F32)
    belongs = jnp.where(whose == owner_row, 1.0, 0.0).astype(BF16)
    slot_lane = lax.broadcasted_iota(jnp.int32, (requests, LANES), 1).astype(F32)
    ranked = jnp.where(slot_lane == rank, inside, 0.0).astype(BF16)
    lists_out[...] = dot(belongs, ranked).reshape(owners, 1, LANES)

    here(lists_out.at[me], lists_in.at[me], list_recv.at[0]).start()
    here(lists_out.at[partner], lists_in.at[partner], list_recv.at[0]).start()
    table_copy.wait()
    pl.semaphore_wait(barrier, owners - 1)

    def lend(c):
        cols = pl.ds(starts[c], sizes[c])
        return there(table.at[pl.ds(0, held), cols], table.at[pl.ds(held, held), cols], lend_send.at[0], lend_recv.at[c],
                     *split(partner))

    lend(0).start()

    @pl.loop(1, owners - 1, unroll=5)
    def _(i):
        owner = other(i)
        target, known = server(owner)
        there(lists_out.at[owner], lists_in.at[known], list_send.at[0], list_recv.at[0], *split(target)).start()

    for c in range(1, len(sizes)):
        lend(c).start()
    for copy in (hidden_copy, hg_copy, kg_copy):
        copy.start()
    for start, size in zip(starts, sizes):
        for k, (source, target) in enumerate(((wk_hbm, wk), (wv_hbm, wv))):
            for h in range(heads):
                here(source.at[pl.ds(h * width + start, size), :],
                     target.at[pl.ds(heads * start + h * size, size), :], local_sem.at[5 + k]).start()

    hidden_copy.wait()
    hg_copy.wait()
    kg_copy.wait()
    hidden_squares = jnp.zeros((requests, LANES), F32)
    for c in range(columns // LANES):
        cols = slice(c * LANES, (c + 1) * LANES)
        value = hidden[:, cols].astype(F32)
        hidden_squares += value * value
        scaled[:, cols] = value * (hg[cols] * kg[cols]).reshape(1, LANES)
    hidden_squares = jnp.sum(hidden_squares, axis=1, keepdims=True)

    there(lists_out, lists_in, list_send.at[0], list_recv.at[0], me_p, me_t).wait_recv()
    shape = (owners, slots, LANES)
    diagonal = lax.broadcasted_iota(jnp.int32, shape, 1) == lax.broadcasted_iota(jnp.int32, shape, 2)
    wanted = jnp.sum(jnp.where(diagonal, jnp.broadcast_to(lists_in[...], shape), 0.0), axis=2, keepdims=True)
    wanted = wanted.reshape(owners * slots, 1)
    whom = lax.broadcasted_iota(jnp.int32, (owners * slots, 1), 0) // slots
    wanted = wanted + jnp.where(((whom ^ me) & side) != 0, float(held), 0.0)
    choose = jnp.where(
        lax.broadcasted_iota(jnp.int32, (owners * slots, 2 * held), 1).astype(F32) == wanted, 1.0, 0.0).astype(BF16)

    for c, (start, size) in enumerate(zip(starts, sizes)):
        cols = pl.ds(start, size)
        lend(c).wait_recv()
        block = dot(choose, table[:, cols])
        sending[:, :, cols] = block.reshape(owners, slots, size).astype(BF16)
        for owner in (me, partner):
            here(sending.at[owner, :, cols], rows.at[owner, :, cols], row_recv.at[c]).start()

        @pl.loop(1, owners - 1, unroll=5)
        def _(i):
            place_of = other(1 + lax.rem(i + owners // 2 - 1, owners - 2))
            away = jnp.where(((me ^ place_of) & side) != 0, way, 0)
            there(sending.at[place_of, :, cols], rows.at[me ^ away, :, cols], row_send.at[0], row_recv.at[c],
                  *split(place_of ^ away)).start()

    def blocks(c):
        return pl.ds(starts[c] // LANES, sizes[c] // LANES)

    def share(c, h, m):
        return lambda n: there(mem.at[h, blocks(c)], mem.at[h, blocks(c)], pass_send.at[0],
                               pass_recv.at[c * (heads - 1) + n - 1], me_p, me_t ^ m)

    def arrived(c, n):
        return there(mem.at[me_t ^ n, blocks(c)], mem.at[me_t ^ n, blocks(c)], pass_send.at[0],
                     pass_recv.at[c * (heads - 1) + n - 1], me_p, me_t ^ n)

    def relayed(c):
        return c != last

    def compact(c):
        cols = pl.ds(starts[c], sizes[c])
        there(sending.at[:, :, cols], rows.at[:, :, cols], row_send.at[0], row_recv.at[c], me_p, me_t).wait_recv()
        mine = dot(place[...], rows[:, :, cols].reshape(owners * slots, sizes[c])).astype(BF16)
        for b in range(sizes[c] // LANES):
            mem[me_t, starts[c] // LANES + b] = mine[:, b * LANES:(b + 1) * LANES]
        for m in list(range(2, heads)) + [1]:
            if m % 2 == 0 or m == 1 or not relayed(c):
                share(c, me_t, m)(m).start()

    def relay(c):
        if relayed(c):
            for m in range(2, heads, 2):
                arrived(c, m).wait_recv()
                share(c, me_t ^ m, 1)(m | 1).start()

    def operand(c, base, count):
        b0, nb = starts[c] // LANES, sizes[c] // LANES
        return jnp.concatenate([mem[base + h, b0 + b] for h in range(count) for b in range(nb)], axis=1)

    def multiply(c, w, acc, base, count):
        x = operand(c, base, count)
        first = heads * starts[c] + base * sizes[c]
        if not isinstance(first, int):
            first = pl.multiple_of(first, LANES)
        depth = pl.ds(first, count * sizes[c])
        for n in range(columns // part):
            cols = pl.ds(n * part, part)
            value = dot(x, w[depth, cols])
            acc[:, cols] = value if c == 0 else acc[:, cols] + value

    def gathered(c):
        for m in range(1, heads):
            if not relayed(c) or m % 2:
                arrived(c, m).wait_recv()

    for c in range(last + 1):
        compact(c)
        if c >= 2:
            if c == 2:
                here(wk_hbm, wk, local_sem.at[5]).wait()
                here(wv_hbm, wv, local_sem.at[6]).wait()
            gathered(c - 2)
            multiply(c - 2, wk, acc_k, 0, heads)
            multiply(c - 2, wv, acc_v, 0, heads)
        if c >= 1:
            relay(c - 1)
    gathered(last - 1)
    multiply(last - 1, wk, acc_k, 0, heads)

    pair = me_t - lax.rem(me_t, 2)
    arrived(last, 1).wait_recv()
    multiply(last, wk, acc_k, pair, 2)
    for m in range(2, heads, 2):
        arrived(last, m).wait_recv()
        arrived(last, m + 1).wait_recv()
        multiply(last, wk, acc_k, pair ^ m, 2)

    key_squares = jnp.zeros((requests, LANES), F32)
    crossing = jnp.zeros((requests, LANES), F32)
    for c in range(columns // LANES):
        cols = slice(c * LANES, (c + 1) * LANES)
        key = acc_k[:, cols]
        key_squares += key * key
        crossing += scaled[:, cols] * key
    key_squares = jnp.sum(key_squares, axis=1, keepdims=True)
    crossing = jnp.sum(crossing, axis=1, keepdims=True)
    lanes = lax.broadcasted_iota(jnp.int32, (requests, LANES), 1)
    packed = jnp.where(lanes == 0, hidden_squares, jnp.where(lanes == 1, key_squares,
                       jnp.where(lanes == 2, crossing, 0.0)))
    stats[0] = packed.T[:8]
    for m in range(heads - 1, 0, -1):
        there(stats.at[0], stats.at[m], stat_send.at[0], stat_recv.at[0], me_p, me_t ^ m).start()

    multiply(last - 1, wv, acc_v, 0, heads)
    multiply(last, wv, acc_v, 0, heads)

    others = there(stats.at[pl.ds(1, heads - 1)], stats.at[pl.ds(1, heads - 1)], stat_send.at[0], stat_recv.at[0],
                   me_p, me_t)
    others.wait_recv()
    summed = stats[0]
    for m in range(1, heads):
        summed += stats[m]
    hidden_total, key_total, cross_total = summed[0:1], summed[1:2], summed[2:3]
    agreement = (cross_total * lax.rsqrt(hidden_total / model + epsilon)
                 * lax.rsqrt(key_total / model + epsilon))
    gate = jax.nn.sigmoid(agreement / math.sqrt(model))
    gate = jnp.broadcast_to(gate, (LANES, requests)).T
    for c in range(columns // LANES):
        cols = slice(c * LANES, (c + 1) * LANES)
        out_ref[:, cols] = (hidden[:, cols].astype(F32) + gate * acc_v[:, cols]).astype(BF16)

    some = pl.ds(0, owners - 2)
    there(lists_out.at[some], lists_in.at[some], list_send.at[0], list_recv.at[0], me_p, me_t).wait_send()
    there(sending.at[some], rows.at[some], row_send.at[0], row_recv.at[0], me_p, me_t).wait_send()
    there(table.at[pl.ds(0, held)], table.at[pl.ds(held, held)], lend_send.at[0], lend_recv.at[0], me_p, me_t).wait_send()
    few = pl.ds(0, heads - 1)
    there(mem.at[few], mem.at[few], pass_send.at[0], pass_recv.at[0], me_p, me_t).wait_send()
    others.wait_send()


def local(groups, heads, hidden, hash_rows, memory_table, key_weight, value_weight, hidden_gain, key_gain):
    requests, columns = hidden.shape
    held, width = memory_table.shape
    owners = groups * heads
    assert hash_rows.shape[1] == 1 and heads & (heads - 1) == 0 and heads > 1
    assert groups & (groups - 1) == 0 and requests == LANES and groups >= 4 and heads >= 4
    slots = max(8, 2 * max(1, hash_rows.size // owners))
    sizes = []
    left = width - LANES
    while left > 0:
        sizes.append(min(2 * LANES, left))
        left -= sizes[-1]
    sizes.append(LANES)
    any_space = pl.BlockSpec(memory_space=pl.ANY)
    vmem = pl.BlockSpec(memory_space=pltpu.VMEM)
    dma = pltpu.SemaphoreType.DMA
    return pl.pallas_call(
        functools.partial(kernel, groups, heads, slots, tuple(sizes)),
        out_shape=jax.ShapeDtypeStruct((requests, columns), BF16),
        in_specs=[any_space] * 7,
        out_specs=vmem,
        scratch_shapes=[
            pltpu.VMEM((1, 1, requests), jnp.int32),
            pltpu.VMEM((columns,), F32),
            pltpu.VMEM((columns,), F32),
            pltpu.VMEM((2 * held, width), BF16),
            pltpu.VMEM((requests, columns), BF16),
            pltpu.VMEM((requests, columns), F32),
            pltpu.VMEM((heads * width, columns), BF16),
            pltpu.VMEM((heads * width, columns), BF16),
            pltpu.VMEM((owners, 1, LANES), F32),
            pltpu.VMEM((owners, 1, LANES), F32),
            pltpu.VMEM((owners, slots, width), BF16),
            pltpu.VMEM((owners, slots, width), BF16),
            pltpu.VMEM((requests, owners * slots), BF16),
            pltpu.VMEM((heads, width // LANES, requests, LANES), BF16),
            pltpu.VMEM((requests, columns), F32),
            pltpu.VMEM((requests, columns), F32),
            pltpu.VMEM((heads, 8, requests), F32),
            dma((7,)), dma((1,)), dma((1,)), dma((1,)), dma((len(sizes),)),
            dma((1,)), dma((len(sizes) * (heads - 1),)), dma((1,)), dma((1,)),
            dma((1,)), dma((len(sizes),)),
        ],
        compiler_params=pltpu.CompilerParams(
            collective_id=0, has_side_effects=True, vmem_limit_bytes=44 * 1024 * 1024),
    )(*(pltpu.with_memory_space_constraint(x, pltpu.HBM) for x in (
        hash_rows.reshape(1, 1, requests), hidden_gain, key_gain, memory_table, hidden, key_weight, value_weight)))


def solution(mesh):
    return jax.shard_map(
        functools.partial(local, mesh.shape["dp"], mesh.shape["tensor"]),
        mesh=mesh,
        in_specs=(
            P("dp", "tensor"),
            P("dp", "tensor"),
            P(("dp", "tensor"), None),
            P(None, "tensor"),
            P(None, "tensor"),
            P("tensor"),
            P("tensor"),
        ),
        out_specs=P("dp", "tensor"),
        check_vma=False,
    )
```

```python
import functools
import math

import jax
import jax.numpy as jnp
from jax import lax
from jax.experimental import pallas as pl
from jax.experimental.pallas import tpu as pltpu
from jax.sharding import PartitionSpec as P

MESH = pl.DeviceIdType.MESH
epsilon = 1e-06
F32, BF16 = jnp.float32, jnp.bfloat16
LANES = 128


def dot(a, b):
    return jnp.dot(a, b, preferred_element_type=F32)


def kernel(groups, heads, slots, sizes, ids_hbm, hg_hbm, kg_hbm, table_hbm, hidden_hbm, wk_hbm, wv_hbm, out_ref,
           ids, hg, kg, table, hidden, scaled, wk, wv, lists_out, lists_in, sending, rows, place, mem, acc_k, acc_v,
           stats, local_sem, list_send, list_recv, row_send, row_recv, pass_send, pass_recv, stat_send, stat_recv,
           lend_send, lend_recv):
    me_p, me_t = lax.axis_index("dp"), lax.axis_index("tensor")
    me = me_p * heads + me_t
    owners = groups * heads
    held, width = table_hbm.shape
    requests, columns = hidden.shape
    model = columns * heads
    part = 256 if columns % 256 == 0 else 128
    starts = [sum(sizes[:c]) for c in range(len(sizes))]
    last = len(sizes) - 1

    def here(source, target, sem):
        return pltpu.make_async_copy(source, target, sem)

    def there(source, target, send, recv, p, t):
        return pltpu.make_async_remote_copy(
            src_ref=source, dst_ref=target, send_sem=send, recv_sem=recv,
            device_id={"dp": p, "tensor": t}, device_id_type=MESH)

    head_bits = heads.bit_length() - 1

    def split(device):
        return device >> head_bits, device & (heads - 1)

    def peer(i):
        return split(me ^ (owners - i))

    across, low, high, quarter = heads // 2, heads, owners // 2, owners // 4

    def pairing(device):
        even = (device & 1) == 0
        middle = ((device + quarter) & high) != 0
        return (jnp.where(even, across, jnp.where(middle, high + quarter, low)),
                jnp.where(even, across, jnp.where(middle, high, low)))

    way, side = pairing(me)
    partner = me ^ way

    def other(i):
        j = owners - i
        return me ^ jnp.where(j > way, j, j - 1)

    def server(owner):
        away, bit = pairing(owner)
        away = jnp.where(((me ^ owner) & bit) != 0, away, 0)
        return owner ^ away, me ^ away

    barrier = pltpu.get_barrier_semaphore()

    ids_copy = here(ids_hbm, ids, local_sem.at[0])
    table_copy = here(table_hbm, table.at[pl.ds(0, held)], local_sem.at[1])
    hidden_copy = here(hidden_hbm, hidden, local_sem.at[2])
    hg_copy = here(hg_hbm, hg, local_sem.at[3])
    kg_copy = here(kg_hbm, kg, local_sem.at[4])
    ids_copy.start()
    table_copy.start()

    @pl.loop(1, owners, unroll=owners - 1)
    def _(i):
        p, t = peer(i)
        pl.semaphore_signal(barrier, inc=1, device_id={"dp": p, "tensor": t}, device_id_type=MESH)


    ids_copy.wait()
    sub = lax.broadcasted_iota(jnp.int32, (requests, requests), 0)
    lane = lax.broadcasted_iota(jnp.int32, (requests, requests), 1)
    numbers = ids[0].astype(F32)
    owner_row = jnp.floor((numbers + 0.5) * (1.0 / held))
    local_row = numbers - owner_row * held
    owner = jnp.broadcast_to(owner_row, (requests, requests))
    column = jnp.sum(jnp.where(sub == lane, owner, 0.0), axis=1, keepdims=True)
    inside = jnp.sum(jnp.where(sub == lane, jnp.broadcast_to(local_row, (requests, requests)), 0.0), axis=1, keepdims=True)
    rank = jnp.sum(jnp.where((owner == column) & (lane < sub), 1.0, 0.0), axis=1, keepdims=True)
    whose = lax.broadcasted_iota(jnp.int32, (owners, requests), 0).astype(F32)
    belongs = jnp.where(whose == owner_row, 1.0, 0.0).astype(BF16)
    slot_lane = lax.broadcasted_iota(jnp.int32, (requests, LANES), 1).astype(F32)
    ranked = jnp.where(slot_lane == rank, inside, 0.0).astype(BF16)
    lists_out[...] = dot(belongs, ranked).reshape(owners, 1, LANES)

    here(lists_out.at[me], lists_in.at[me], list_recv.at[0]).start()
    here(lists_out.at[partner], lists_in.at[partner], list_recv.at[0]).start()
    table_copy.wait()
    pl.semaphore_wait(barrier, owners - 1)

    def lend(c):
        cols = pl.ds(starts[c], sizes[c])
        return there(table.at[pl.ds(0, held), cols], table.at[pl.ds(held, held), cols], lend_send.at[0], lend_recv.at[c],
                     *split(partner))

    @pl.loop(1, owners // 2, unroll=10)
    def _(i):
        owner = other(i)
        target, known = server(owner)
        there(lists_out.at[owner], lists_in.at[known], list_send.at[0], list_recv.at[0], *split(target)).start()

    lend(0).start()

    @pl.loop(owners // 2, owners - 1, unroll=10)
    def _(i):
        owner = other(i)
        target, known = server(owner)
        there(lists_out.at[owner], lists_in.at[known], list_send.at[0], list_recv.at[0], *split(target)).start()

    for c in range(1, len(sizes)):
        lend(c).start()
    for copy in (hidden_copy, hg_copy, kg_copy):
        copy.start()
    for start, size in zip(starts, sizes):
        for k, (source, target) in enumerate(((wk_hbm, wk), (wv_hbm, wv))):
            for h in range(heads):
                here(source.at[pl.ds(h * width + start, size), :],
                     target.at[pl.ds(heads * start + h * size, size), :], local_sem.at[5 + k]).start()

    spots = lax.broadcasted_iota(jnp.int32, (requests, owners * slots), 1).astype(F32)
    place[...] = jnp.where(spots == column * slots + rank, 1.0, 0.0).astype(BF16)

    hidden_copy.wait()
    hg_copy.wait()
    kg_copy.wait()
    hidden_squares = jnp.zeros((requests, LANES), F32)
    for c in range(columns // LANES):
        cols = slice(c * LANES, (c + 1) * LANES)
        value = hidden[:, cols].astype(F32)
        hidden_squares += value * value
        scaled[:, cols] = value * (hg[cols] * kg[cols]).reshape(1, LANES)
    hidden_squares = jnp.sum(hidden_squares, axis=1, keepdims=True)

    there(lists_out, lists_in, list_send.at[0], list_recv.at[0], me_p, me_t).wait_recv()
    shape = (owners, slots, LANES)
    diagonal = lax.broadcasted_iota(jnp.int32, shape, 1) == lax.broadcasted_iota(jnp.int32, shape, 2)
    wanted = jnp.sum(jnp.where(diagonal, jnp.broadcast_to(lists_in[...], shape), 0.0), axis=2, keepdims=True)
    wanted = wanted.reshape(owners * slots, 1)
    whom = lax.broadcasted_iota(jnp.int32, (owners * slots, 1), 0) // slots
    wanted = wanted + jnp.where(((whom ^ me) & side) != 0, float(held), 0.0)
    choose = jnp.where(
        lax.broadcasted_iota(jnp.int32, (owners * slots, 2 * held), 1).astype(F32) == wanted, 1.0, 0.0).astype(BF16)

    for c, (start, size) in enumerate(zip(starts, sizes)):
        cols = pl.ds(start, size)
        lend(c).wait_recv()
        block = dot(choose, table[:, cols])
        sending[:, :, cols] = block.reshape(owners, slots, size).astype(BF16)
        for owner in (me, partner):
            here(sending.at[owner, :, cols], rows.at[owner, :, cols], row_recv.at[c]).start()

        @pl.loop(1, owners - 1, unroll=10)
        def _(i):
            place_of = other(1 + lax.rem(i + owners // 2 - 1, owners - 2))
            away = jnp.where(((me ^ place_of) & side) != 0, way, 0)
            there(sending.at[place_of, :, cols], rows.at[me ^ away, :, cols], row_send.at[0], row_recv.at[c],
                  *split(place_of ^ away)).start()

    def blocks(c):
        return pl.ds(starts[c] // LANES, sizes[c] // LANES)

    def share(c, h, m):
        return lambda n: there(mem.at[h, blocks(c)], mem.at[h, blocks(c)], pass_send.at[0],
                               pass_recv.at[c * (heads - 1) + n - 1], me_p, me_t ^ m)

    def arrived(c, n):
        return there(mem.at[me_t ^ n, blocks(c)], mem.at[me_t ^ n, blocks(c)], pass_send.at[0],
                     pass_recv.at[c * (heads - 1) + n - 1], me_p, me_t ^ n)

    def relayed(c):
        return c != last

    def compact(c):
        cols = pl.ds(starts[c], sizes[c])
        there(sending.at[:, :, cols], rows.at[:, :, cols], row_send.at[0], row_recv.at[c], me_p, me_t).wait_recv()
        mine = dot(place[...], rows[:, :, cols].reshape(owners * slots, sizes[c])).astype(BF16)
        for b in range(sizes[c] // LANES):
            mem[me_t, starts[c] // LANES + b] = mine[:, b * LANES:(b + 1) * LANES]
        for m in list(range(2, heads)) + [1]:
            if m % 2 == 1 or not relayed(c):
                share(c, me_t, m)(m).start()

    def relay(c):
        if relayed(c):
            for m in range(3, heads, 2):
                arrived(c, m).wait_recv()
                share(c, me_t ^ m, 1)(m ^ 1).start()

    def operand(c, base, count):
        b0, nb = starts[c] // LANES, sizes[c] // LANES
        return jnp.concatenate([mem[base + h, b0 + b] for h in range(count) for b in range(nb)], axis=1)

    def multiply(c, w, acc, base, count):
        x = operand(c, base, count)
        first = heads * starts[c] + base * sizes[c]
        if not isinstance(first, int):
            first = pl.multiple_of(first, LANES)
        depth = pl.ds(first, count * sizes[c])
        for n in range(columns // part):
            cols = pl.ds(n * part, part)
            value = dot(x, w[depth, cols])
            acc[:, cols] = value if c == 0 else acc[:, cols] + value

    def gathered(c):
        for m in range(1, heads):
            if not relayed(c) or m % 2 == 0 or m == 1:
                arrived(c, m).wait_recv()

    for c in range(last + 1):
        compact(c)
        if c >= 2:
            if c == 2:
                here(wk_hbm, wk, local_sem.at[5]).wait()
                here(wv_hbm, wv, local_sem.at[6]).wait()
            gathered(c - 2)
            multiply(c - 2, wk, acc_k, 0, heads)
            multiply(c - 2, wv, acc_v, 0, heads)
        if c >= 1:
            relay(c - 1)
    gathered(last - 1)
    multiply(last - 1, wk, acc_k, 0, heads)

    pair = me_t - lax.rem(me_t, 2)
    arrived(last, 1).wait_recv()
    multiply(last, wk, acc_k, pair, 2)
    for m in range(2, heads, 2):
        arrived(last, m).wait_recv()
        arrived(last, m + 1).wait_recv()
        multiply(last, wk, acc_k, pair ^ m, 2)

    key_squares = jnp.zeros((requests, LANES), F32)
    crossing = jnp.zeros((requests, LANES), F32)
    for c in range(columns // LANES):
        cols = slice(c * LANES, (c + 1) * LANES)
        key = acc_k[:, cols]
        key_squares += key * key
        crossing += scaled[:, cols] * key
    key_squares = jnp.sum(key_squares, axis=1, keepdims=True)
    crossing = jnp.sum(crossing, axis=1, keepdims=True)
    lanes = lax.broadcasted_iota(jnp.int32, (requests, LANES), 1)
    packed = jnp.where(lanes == 0, hidden_squares, jnp.where(lanes == 1, key_squares,
                       jnp.where(lanes == 2, crossing, 0.0)))
    stats[0] = packed.T[:8]
    for m in range(heads - 1, 0, -1):
        there(stats.at[0], stats.at[m], stat_send.at[0], stat_recv.at[0], me_p, me_t ^ m).start()

    multiply(last - 1, wv, acc_v, 0, heads)
    multiply(last, wv, acc_v, 0, heads)

    others = there(stats.at[pl.ds(1, heads - 1)], stats.at[pl.ds(1, heads - 1)], stat_send.at[0], stat_recv.at[0],
                   me_p, me_t)
    others.wait_recv()
    summed = stats[0]
    for m in range(1, heads):
        summed += stats[m]
    hidden_total, key_total, cross_total = summed[0:1], summed[1:2], summed[2:3]
    agreement = (cross_total * lax.rsqrt(hidden_total / model + epsilon)
                 * lax.rsqrt(key_total / model + epsilon))
    gate = jax.nn.sigmoid(agreement / math.sqrt(model))
    gate = jnp.broadcast_to(gate, (LANES, requests)).T
    for c in range(columns // LANES):
        cols = slice(c * LANES, (c + 1) * LANES)
        out_ref[:, cols] = (hidden[:, cols].astype(F32) + gate * acc_v[:, cols]).astype(BF16)

    some = pl.ds(0, owners - 2)
    there(lists_out.at[some], lists_in.at[some], list_send.at[0], list_recv.at[0], me_p, me_t).wait_send()
    there(sending.at[some], rows.at[some], row_send.at[0], row_recv.at[0], me_p, me_t).wait_send()
    there(table.at[pl.ds(0, held)], table.at[pl.ds(held, held)], lend_send.at[0], lend_recv.at[0], me_p, me_t).wait_send()
    few = pl.ds(0, heads - 1)
    there(mem.at[few], mem.at[few], pass_send.at[0], pass_recv.at[0], me_p, me_t).wait_send()
    others.wait_send()


def local(groups, heads, hidden, hash_rows, memory_table, key_weight, value_weight, hidden_gain, key_gain):
    requests, columns = hidden.shape
    held, width = memory_table.shape
    owners = groups * heads
    assert hash_rows.shape[1] == 1 and heads & (heads - 1) == 0 and heads > 1
    assert groups & (groups - 1) == 0 and requests == LANES and groups >= 4 and heads >= 4
    slots = max(8, 2 * max(1, hash_rows.size // owners))
    sizes = []
    left = width - LANES
    while left > 0:
        sizes.append(min(2 * LANES, left))
        left -= sizes[-1]
    sizes.append(LANES)
    any_space = pl.BlockSpec(memory_space=pl.ANY)
    vmem = pl.BlockSpec(memory_space=pltpu.VMEM)
    dma = pltpu.SemaphoreType.DMA
    return pl.pallas_call(
        functools.partial(kernel, groups, heads, slots, tuple(sizes)),
        out_shape=jax.ShapeDtypeStruct((requests, columns), BF16),
        in_specs=[any_space] * 7,
        out_specs=vmem,
        scratch_shapes=[
            pltpu.VMEM((1, 1, requests), jnp.int32),
            pltpu.VMEM((columns,), F32),
            pltpu.VMEM((columns,), F32),
            pltpu.VMEM((2 * held, width), BF16),
            pltpu.VMEM((requests, columns), BF16),
            pltpu.VMEM((requests, columns), F32),
            pltpu.VMEM((heads * width, columns), BF16),
            pltpu.VMEM((heads * width, columns), BF16),
            pltpu.VMEM((owners, 1, LANES), F32),
            pltpu.VMEM((owners, 1, LANES), F32),
            pltpu.VMEM((owners, slots, width), BF16),
            pltpu.VMEM((owners, slots, width), BF16),
            pltpu.VMEM((requests, owners * slots), BF16),
            pltpu.VMEM((heads, width // LANES, requests, LANES), BF16),
            pltpu.VMEM((requests, columns), F32),
            pltpu.VMEM((requests, columns), F32),
            pltpu.VMEM((heads, 8, requests), F32),
            dma((7,)), dma((1,)), dma((1,)), dma((1,)), dma((len(sizes),)),
            dma((1,)), dma((len(sizes) * (heads - 1),)), dma((1,)), dma((1,)),
            dma((1,)), dma((len(sizes),)),
        ],
        compiler_params=pltpu.CompilerParams(
            collective_id=0, has_side_effects=True, vmem_limit_bytes=44 * 1024 * 1024),
    )(*(pltpu.with_memory_space_constraint(x, pltpu.HBM) for x in (
        hash_rows.reshape(1, 1, requests), hidden_gain, key_gain, memory_table, hidden, key_weight, value_weight)))


def solution(mesh):
    return jax.shard_map(
        functools.partial(local, mesh.shape["dp"], mesh.shape["tensor"]),
        mesh=mesh,
        in_specs=(
            P("dp", "tensor"),
            P("dp", "tensor"),
            P(("dp", "tensor"), None),
            P(None, "tensor"),
            P(None, "tensor"),
            P("tensor"),
            P("tensor"),
        ),
        out_specs=P("dp", "tensor"),
        check_vma=False,
    )
```

```python
import functools
import math

import jax
import jax.numpy as jnp
from jax import lax
from jax.experimental import pallas as pl
from jax.experimental.pallas import tpu as pltpu
from jax.sharding import PartitionSpec as P

MESH = pl.DeviceIdType.MESH
epsilon = 1e-06
F32, BF16 = jnp.float32, jnp.bfloat16
LANES = 128


def dot(a, b):
    return jnp.dot(a, b, preferred_element_type=F32)


def kernel(groups, heads, slots, sizes, ids_hbm, hg_hbm, kg_hbm, table_hbm, hidden_hbm, wk_hbm, wv_hbm, out_ref,
           ids, hg, kg, table, hidden, scaled, wk, wv, lists_out, lists_in, sending, rows, place, mem, acc_k, acc_v,
           stats, local_sem, list_send, list_recv, row_send, row_recv, pass_send, pass_recv, stat_send, stat_recv,
           lend_send, lend_recv):
    me_p, me_t = lax.axis_index("dp"), lax.axis_index("tensor")
    me = me_p * heads + me_t
    owners = groups * heads
    held, width = table_hbm.shape
    requests, columns = hidden.shape
    model = columns * heads
    part = 256 if columns % 256 == 0 else 128
    starts = [sum(sizes[:c]) for c in range(len(sizes))]
    last = len(sizes) - 1

    def here(source, target, sem):
        return pltpu.make_async_copy(source, target, sem)

    def there(source, target, send, recv, p, t):
        return pltpu.make_async_remote_copy(
            src_ref=source, dst_ref=target, send_sem=send, recv_sem=recv,
            device_id={"dp": p, "tensor": t}, device_id_type=MESH)

    head_bits = heads.bit_length() - 1

    def split(device):
        return device >> head_bits, device & (heads - 1)

    def peer(i):
        return split(me ^ (owners - i))

    across, low, high, quarter = heads // 2, heads, owners // 2, owners // 4

    def pairing(device):
        even = (device & 1) == 0
        middle = ((device + quarter) & high) != 0
        return (jnp.where(even, across, jnp.where(middle, high + quarter, low)),
                jnp.where(even, across, jnp.where(middle, high, low)))

    way, side = pairing(me)
    partner = me ^ way

    def other(i):
        j = owners - i
        return me ^ jnp.where(j > way, j, j - 1)

    def server(owner):
        away, bit = pairing(owner)
        away = jnp.where(((me ^ owner) & bit) != 0, away, 0)
        return owner ^ away, me ^ away

    barrier = pltpu.get_barrier_semaphore()

    ids_copy = here(ids_hbm, ids, local_sem.at[0])
    table_copy = here(table_hbm, table.at[pl.ds(0, held)], local_sem.at[1])
    hidden_copy = here(hidden_hbm, hidden, local_sem.at[2])
    hg_copy = here(hg_hbm, hg, local_sem.at[3])
    kg_copy = here(kg_hbm, kg, local_sem.at[4])
    ids_copy.start()
    table_copy.start()

    @pl.loop(1, owners, unroll=owners - 1)
    def _(i):
        p, t = peer(i)
        pl.semaphore_signal(barrier, inc=1, device_id={"dp": p, "tensor": t}, device_id_type=MESH)


    ids_copy.wait()
    sub = lax.broadcasted_iota(jnp.int32, (requests, requests), 0)
    lane = lax.broadcasted_iota(jnp.int32, (requests, requests), 1)
    numbers = ids[0].astype(F32)
    owner_row = jnp.floor((numbers + 0.5) * (1.0 / held))
    local_row = numbers - owner_row * held
    owner = jnp.broadcast_to(owner_row, (requests, requests))
    column = jnp.sum(jnp.where(sub == lane, owner, 0.0), axis=1, keepdims=True)
    inside = jnp.sum(jnp.where(sub == lane, jnp.broadcast_to(local_row, (requests, requests)), 0.0), axis=1, keepdims=True)
    rank = jnp.sum(jnp.where((owner == column) & (lane < sub), 1.0, 0.0), axis=1, keepdims=True)
    whose = lax.broadcasted_iota(jnp.int32, (owners, requests), 0).astype(F32)
    belongs = jnp.where(whose == owner_row, 1.0, 0.0).astype(BF16)
    slot_lane = lax.broadcasted_iota(jnp.int32, (requests, LANES), 1).astype(F32)
    ranked = jnp.where(slot_lane == rank, inside, 0.0).astype(BF16)
    lists_out[...] = dot(belongs, ranked).reshape(owners, 1, LANES)

    here(lists_out.at[me], lists_in.at[me], list_recv.at[0]).start()
    here(lists_out.at[partner], lists_in.at[partner], list_recv.at[0]).start()
    table_copy.wait()
    pl.semaphore_wait(barrier, owners - 1)

    def lend(c):
        cols = pl.ds(starts[c], sizes[c])
        return there(table.at[pl.ds(0, held), cols], table.at[pl.ds(held, held), cols], lend_send.at[0], lend_recv.at[c],
                     *split(partner))

    @pl.loop(1, owners // 2, unroll=10)
    def _(i):
        owner = other(i)
        target, known = server(owner)
        there(lists_out.at[owner], lists_in.at[known], list_send.at[0], list_recv.at[0], *split(target)).start()

    lend(0).start()

    @pl.loop(owners // 2, owners - 1, unroll=10)
    def _(i):
        owner = other(i)
        target, known = server(owner)
        there(lists_out.at[owner], lists_in.at[known], list_send.at[0], list_recv.at[0], *split(target)).start()

    for c in range(1, len(sizes)):
        lend(c).start()
    for copy in (hidden_copy, hg_copy, kg_copy):
        copy.start()
    for start, size in zip(starts, sizes):
        for k, (source, target) in enumerate(((wk_hbm, wk), (wv_hbm, wv))):
            for h in range(heads):
                here(source.at[pl.ds(h * width + start, size), :],
                     target.at[pl.ds(heads * start + h * size, size), :], local_sem.at[5 + k]).start()

    spots = lax.broadcasted_iota(jnp.int32, (requests, owners * slots), 1).astype(F32)
    place[...] = jnp.where(spots == column * slots + rank, 1.0, 0.0).astype(BF16)

    hidden_copy.wait()
    hg_copy.wait()
    kg_copy.wait()
    hidden_squares = jnp.zeros((requests, LANES), F32)
    for c in range(columns // LANES):
        cols = slice(c * LANES, (c + 1) * LANES)
        value = hidden[:, cols].astype(F32)
        hidden_squares += value * value
        scaled[:, cols] = value * (hg[cols] * kg[cols]).reshape(1, LANES)
    hidden_squares = jnp.sum(hidden_squares, axis=1, keepdims=True)

    there(lists_out, lists_in, list_send.at[0], list_recv.at[0], me_p, me_t).wait_recv()
    shape = (owners, slots, LANES)
    diagonal = lax.broadcasted_iota(jnp.int32, shape, 1) == lax.broadcasted_iota(jnp.int32, shape, 2)
    wanted = jnp.sum(jnp.where(diagonal, jnp.broadcast_to(lists_in[...], shape), 0.0), axis=2, keepdims=True)
    wanted = wanted.reshape(owners * slots, 1)
    whom = lax.broadcasted_iota(jnp.int32, (owners * slots, 1), 0) // slots
    wanted = wanted + jnp.where(((whom ^ me) & side) != 0, float(held), 0.0)
    choose = jnp.where(
        lax.broadcasted_iota(jnp.int32, (owners * slots, 2 * held), 1).astype(F32) == wanted, 1.0, 0.0).astype(BF16)

    for c, (start, size) in enumerate(zip(starts, sizes)):
        cols = pl.ds(start, size)
        lend(c).wait_recv()
        block = dot(choose, table[:, cols])
        sending[:, :, cols] = block.reshape(owners, slots, size).astype(BF16)
        for owner in (me, partner):
            here(sending.at[owner, :, cols], rows.at[owner, :, cols], row_recv.at[c]).start()

        @pl.loop(1, owners - 1, unroll=10)
        def _(i):
            place_of = other(1 + lax.rem(i + owners // 2 - 1, owners - 2))
            away = jnp.where(((me ^ place_of) & side) != 0, way, 0)
            there(sending.at[place_of, :, cols], rows.at[me ^ away, :, cols], row_send.at[0], row_recv.at[c],
                  *split(place_of ^ away)).start()

    def blocks(c):
        return pl.ds(starts[c] // LANES, sizes[c] // LANES)

    def share(c, h, m):
        return lambda n: there(mem.at[h, blocks(c)], mem.at[h, blocks(c)], pass_send.at[0],
                               pass_recv.at[c * (heads - 1) + n - 1], me_p, me_t ^ m)

    def arrived(c, n):
        return there(mem.at[me_t ^ n, blocks(c)], mem.at[me_t ^ n, blocks(c)], pass_send.at[0],
                     pass_recv.at[c * (heads - 1) + n - 1], me_p, me_t ^ n)

    def relayed(c):
        return c != last

    def compact(c):
        cols = pl.ds(starts[c], sizes[c])
        there(sending.at[:, :, cols], rows.at[:, :, cols], row_send.at[0], row_recv.at[c], me_p, me_t).wait_recv()
        mine = dot(place[...], rows[:, :, cols].reshape(owners * slots, sizes[c])).astype(BF16)
        for b in range(sizes[c] // LANES):
            mem[me_t, starts[c] // LANES + b] = mine[:, b * LANES:(b + 1) * LANES]
        for m in list(range(2, heads)) + [1]:
            if m % 2 == 1 or not relayed(c):
                share(c, me_t, m)(m).start()

    def relay(c):
        if relayed(c):
            for m in range(3, heads, 2):
                arrived(c, m).wait_recv()
                share(c, me_t ^ m, 1)(m ^ 1).start()

    def operand(c, base, count):
        b0, nb = starts[c] // LANES, sizes[c] // LANES
        return jnp.concatenate([mem[base + h, b0 + b] for h in range(count) for b in range(nb)], axis=1)

    def multiply(c, w, acc, base, count):
        x = operand(c, base, count)
        first = heads * starts[c] + base * sizes[c]
        if not isinstance(first, int):
            first = pl.multiple_of(first, LANES)
        depth = pl.ds(first, count * sizes[c])
        for n in range(columns // part):
            cols = pl.ds(n * part, part)
            value = dot(x, w[depth, cols])
            acc[:, cols] = value if c == 0 else acc[:, cols] + value

    def gathered(c):
        for m in range(1, heads):
            if not relayed(c) or m % 2 == 0 or m == 1:
                arrived(c, m).wait_recv()

    for c in range(last + 1):
        compact(c)
        if c >= 2:
            if c == 2:
                here(wk_hbm, wk, local_sem.at[5]).wait()
                here(wv_hbm, wv, local_sem.at[6]).wait()
            gathered(c - 2)
            multiply(c - 2, wk, acc_k, 0, heads)
            multiply(c - 2, wv, acc_v, 0, heads)
        if c >= 1:
            relay(c - 1)
    gathered(last - 1)
    multiply(last - 1, wk, acc_k, 0, heads)

    pair = me_t - lax.rem(me_t, 2)
    arrived(last, 1).wait_recv()
    multiply(last, wk, acc_k, pair, 2)
    for m in range(2, heads, 2):
        arrived(last, m).wait_recv()
        arrived(last, m + 1).wait_recv()
        if m + 2 < heads:
            multiply(last, wk, acc_k, pair ^ m, 2)

    key_squares = jnp.zeros((requests, LANES), F32)
    crossing = jnp.zeros((requests, LANES), F32)
    base = pair ^ (heads - 2)
    x = operand(last, base, 2)
    depth = pl.ds(pl.multiple_of(heads * starts[last] + base * sizes[last], LANES), 2 * sizes[last])
    for n in range(columns // part):
        key = acc_k[:, n * part:(n + 1) * part] + dot(x, wk[depth, n * part:(n + 1) * part])
        for b in range(part // LANES):
            one = key[:, b * LANES:(b + 1) * LANES]
            key_squares += one * one
            crossing += scaled[:, n * part + b * LANES:n * part + (b + 1) * LANES] * one
    key_squares = jnp.sum(key_squares, axis=1, keepdims=True)
    crossing = jnp.sum(crossing, axis=1, keepdims=True)
    lanes = lax.broadcasted_iota(jnp.int32, (requests, LANES), 1)
    packed = jnp.where(lanes == 0, hidden_squares, jnp.where(lanes == 1, key_squares,
                       jnp.where(lanes == 2, crossing, 0.0)))
    stats[0] = packed.T[:8]
    for m in range(heads - 1, 0, -1):
        there(stats.at[0], stats.at[m], stat_send.at[0], stat_recv.at[0], me_p, me_t ^ m).start()

    multiply(last - 1, wv, acc_v, 0, heads)
    multiply(last, wv, acc_v, 0, heads)

    others = there(stats.at[pl.ds(1, heads - 1)], stats.at[pl.ds(1, heads - 1)], stat_send.at[0], stat_recv.at[0],
                   me_p, me_t)
    others.wait_recv()
    summed = stats[0]
    for m in range(1, heads):
        summed += stats[m]
    hidden_total, key_total, cross_total = summed[0:1], summed[1:2], summed[2:3]
    agreement = (cross_total * lax.rsqrt(hidden_total / model + epsilon)
                 * lax.rsqrt(key_total / model + epsilon))
    gate = jax.nn.sigmoid(agreement / math.sqrt(model))
    gate = jnp.broadcast_to(gate, (LANES, requests)).T
    for c in range(columns // LANES):
        cols = slice(c * LANES, (c + 1) * LANES)
        out_ref[:, cols] = (hidden[:, cols].astype(F32) + gate * acc_v[:, cols]).astype(BF16)

    some = pl.ds(0, owners - 2)
    there(lists_out.at[some], lists_in.at[some], list_send.at[0], list_recv.at[0], me_p, me_t).wait_send()
    there(sending.at[some], rows.at[some], row_send.at[0], row_recv.at[0], me_p, me_t).wait_send()
    there(table.at[pl.ds(0, held)], table.at[pl.ds(held, held)], lend_send.at[0], lend_recv.at[0], me_p, me_t).wait_send()
    few = pl.ds(0, heads - 1)
    there(mem.at[few], mem.at[few], pass_send.at[0], pass_recv.at[0], me_p, me_t).wait_send()
    others.wait_send()


def local(groups, heads, hidden, hash_rows, memory_table, key_weight, value_weight, hidden_gain, key_gain):
    requests, columns = hidden.shape
    held, width = memory_table.shape
    owners = groups * heads
    assert hash_rows.shape[1] == 1 and heads & (heads - 1) == 0 and heads > 1
    assert groups & (groups - 1) == 0 and requests == LANES and groups >= 4 and heads >= 4
    slots = max(8, 2 * max(1, hash_rows.size // owners))
    sizes = []
    left = width - LANES
    while left > 0:
        sizes.append(min(2 * LANES, left))
        left -= sizes[-1]
    sizes.append(LANES)
    any_space = pl.BlockSpec(memory_space=pl.ANY)
    vmem = pl.BlockSpec(memory_space=pltpu.VMEM)
    dma = pltpu.SemaphoreType.DMA
    return pl.pallas_call(
        functools.partial(kernel, groups, heads, slots, tuple(sizes)),
        out_shape=jax.ShapeDtypeStruct((requests, columns), BF16),
        in_specs=[any_space] * 7,
        out_specs=vmem,
        scratch_shapes=[
            pltpu.VMEM((1, 1, requests), jnp.int32),
            pltpu.VMEM((columns,), F32),
            pltpu.VMEM((columns,), F32),
            pltpu.VMEM((2 * held, width), BF16),
            pltpu.VMEM((requests, columns), BF16),
            pltpu.VMEM((requests, columns), F32),
            pltpu.VMEM((heads * width, columns), BF16),
            pltpu.VMEM((heads * width, columns), BF16),
            pltpu.VMEM((owners, 1, LANES), F32),
            pltpu.VMEM((owners, 1, LANES), F32),
            pltpu.VMEM((owners, slots, width), BF16),
            pltpu.VMEM((owners, slots, width), BF16),
            pltpu.VMEM((requests, owners * slots), BF16),
            pltpu.VMEM((heads, width // LANES, requests, LANES), BF16),
            pltpu.VMEM((requests, columns), F32),
            pltpu.VMEM((requests, columns), F32),
            pltpu.VMEM((heads, 8, requests), F32),
            dma((7,)), dma((1,)), dma((1,)), dma((1,)), dma((len(sizes),)),
            dma((1,)), dma((len(sizes) * (heads - 1),)), dma((1,)), dma((1,)),
            dma((1,)), dma((len(sizes),)),
        ],
        compiler_params=pltpu.CompilerParams(
            collective_id=0, has_side_effects=True, vmem_limit_bytes=44 * 1024 * 1024),
    )(*(pltpu.with_memory_space_constraint(x, pltpu.HBM) for x in (
        hash_rows.reshape(1, 1, requests), hidden_gain, key_gain, memory_table, hidden, key_weight, value_weight)))


def solution(mesh):
    return jax.shard_map(
        functools.partial(local, mesh.shape["dp"], mesh.shape["tensor"]),
        mesh=mesh,
        in_specs=(
            P("dp", "tensor"),
            P("dp", "tensor"),
            P(("dp", "tensor"), None),
            P(None, "tensor"),
            P(None, "tensor"),
            P("tensor"),
            P("tensor"),
        ),
        out_specs=P("dp", "tensor"),
        check_vma=False,
    )
```

```python
import functools
import math

import jax
import jax.numpy as jnp
from jax import lax
from jax.experimental import pallas as pl
from jax.experimental.pallas import tpu as pltpu
from jax.sharding import PartitionSpec as P

MESH = pl.DeviceIdType.MESH
epsilon = 1e-06
F32, BF16 = jnp.float32, jnp.bfloat16
LANES = 128


def dot(a, b):
    return jnp.dot(a, b, preferred_element_type=F32)


def kernel(groups, heads, slots, sizes, ids_hbm, hg_hbm, kg_hbm, table_hbm, hidden_hbm, wk_hbm, wv_hbm, out_ref,
           ids, hg, kg, table, hidden, scaled, wk, wv, lists_out, lists_in, sending, rows, place, mem, acc_k, acc_v,
           stats, local_sem, list_send, list_recv, row_send, row_recv, pass_send, pass_recv, stat_send, stat_recv,
           lend_send, lend_recv):
    me_p, me_t = lax.axis_index("dp"), lax.axis_index("tensor")
    me = me_p * heads + me_t
    owners = groups * heads
    held, width = table_hbm.shape
    requests, columns = hidden.shape
    model = columns * heads
    part = 256 if columns % 256 == 0 else 128
    starts = [sum(sizes[:c]) for c in range(len(sizes))]
    last = len(sizes) - 1

    def here(source, target, sem):
        return pltpu.make_async_copy(source, target, sem)

    def there(source, target, send, recv, p, t):
        return pltpu.make_async_remote_copy(
            src_ref=source, dst_ref=target, send_sem=send, recv_sem=recv,
            device_id={"dp": p, "tensor": t}, device_id_type=MESH)

    head_bits = heads.bit_length() - 1

    def split(device):
        return device >> head_bits, device & (heads - 1)

    def peer(i):
        return split(me ^ (owners - i))

    across, low, high, quarter = heads // 2, heads, owners // 2, owners // 4

    def pairing(device):
        even = (device & 1) == 0
        middle = ((device + quarter) & high) != 0
        return (jnp.where(even, across, jnp.where(middle, high + quarter, low)),
                jnp.where(even, across, jnp.where(middle, high, low)))

    way, side = pairing(me)
    partner = me ^ way

    def other(i):
        j = owners - i
        return me ^ jnp.where(j > way, j, j - 1)

    def server(owner):
        away, bit = pairing(owner)
        away = jnp.where(((me ^ owner) & bit) != 0, away, 0)
        return owner ^ away, me ^ away

    barrier = pltpu.get_barrier_semaphore()

    ids_copy = here(ids_hbm, ids, local_sem.at[0])
    table_copy = here(table_hbm, table.at[pl.ds(0, held)], local_sem.at[1])
    hidden_copy = here(hidden_hbm, hidden, local_sem.at[2])
    hg_copy = here(hg_hbm, hg, local_sem.at[3])
    kg_copy = here(kg_hbm, kg, local_sem.at[4])
    ids_copy.start()
    table_copy.start()

    @pl.loop(1, owners, unroll=owners - 1)
    def _(i):
        p, t = peer(i)
        pl.semaphore_signal(barrier, inc=1, device_id={"dp": p, "tensor": t}, device_id_type=MESH)


    ids_copy.wait()
    sub = lax.broadcasted_iota(jnp.int32, (requests, requests), 0)
    lane = lax.broadcasted_iota(jnp.int32, (requests, requests), 1)
    numbers = ids[0].astype(F32)
    owner_row = jnp.floor((numbers + 0.5) * (1.0 / held))
    local_row = numbers - owner_row * held
    owner = jnp.broadcast_to(owner_row, (requests, requests))
    column = jnp.sum(jnp.where(sub == lane, owner, 0.0), axis=1, keepdims=True)
    inside = jnp.sum(jnp.where(sub == lane, jnp.broadcast_to(local_row, (requests, requests)), 0.0), axis=1, keepdims=True)
    rank = jnp.sum(jnp.where((owner == column) & (lane < sub), 1.0, 0.0), axis=1, keepdims=True)
    whose = lax.broadcasted_iota(jnp.int32, (owners, requests), 0).astype(F32)
    belongs = jnp.where(whose == owner_row, 1.0, 0.0).astype(BF16)
    slot_lane = lax.broadcasted_iota(jnp.int32, (requests, LANES), 1).astype(F32)
    ranked = jnp.where(slot_lane == rank, inside, 0.0).astype(BF16)
    lists_out[...] = dot(belongs, ranked).reshape(owners, 1, LANES)

    here(lists_out.at[me], lists_in.at[me], list_recv.at[0]).start()
    here(lists_out.at[partner], lists_in.at[partner], list_recv.at[0]).start()
    pl.semaphore_wait(barrier, owners - 1)

    def lend(c):
        cols = pl.ds(starts[c], sizes[c])
        return there(table.at[pl.ds(0, held), cols], table.at[pl.ds(held, held), cols], lend_send.at[0], lend_recv.at[c],
                     *split(partner))

    @pl.loop(1, owners // 2, unroll=10)
    def _(i):
        owner = other(i)
        target, known = server(owner)
        there(lists_out.at[owner], lists_in.at[known], list_send.at[0], list_recv.at[0], *split(target)).start()

    table_copy.wait()
    lend(0).start()

    @pl.loop(owners // 2, owners - 1, unroll=10)
    def _(i):
        owner = other(i)
        target, known = server(owner)
        there(lists_out.at[owner], lists_in.at[known], list_send.at[0], list_recv.at[0], *split(target)).start()

    for c in range(1, len(sizes)):
        lend(c).start()
    for copy in (hidden_copy, hg_copy, kg_copy):
        copy.start()
    for start, size in zip(starts, sizes):
        for k, (source, target) in enumerate(((wk_hbm, wk), (wv_hbm, wv))):
            for h in range(heads):
                here(source.at[pl.ds(h * width + start, size), :],
                     target.at[pl.ds(heads * start + h * size, size), :], local_sem.at[5 + k]).start()

    spots = lax.broadcasted_iota(jnp.int32, (requests, owners * slots), 1).astype(F32)
    place[...] = jnp.where(spots == column * slots + rank, 1.0, 0.0).astype(BF16)

    hidden_copy.wait()
    hg_copy.wait()
    kg_copy.wait()
    hidden_squares = jnp.zeros((requests, LANES), F32)
    for c in range(columns // LANES):
        cols = slice(c * LANES, (c + 1) * LANES)
        value = hidden[:, cols].astype(F32)
        hidden_squares += value * value
        scaled[:, cols] = value * (hg[cols] * kg[cols]).reshape(1, LANES)
    hidden_squares = jnp.sum(hidden_squares, axis=1, keepdims=True)

    there(lists_out, lists_in, list_send.at[0], list_recv.at[0], me_p, me_t).wait_recv()
    shape = (owners, slots, LANES)
    diagonal = lax.broadcasted_iota(jnp.int32, shape, 1) == lax.broadcasted_iota(jnp.int32, shape, 2)
    wanted = jnp.sum(jnp.where(diagonal, jnp.broadcast_to(lists_in[...], shape), 0.0), axis=2, keepdims=True)
    wanted = wanted.reshape(owners * slots, 1)
    whom = lax.broadcasted_iota(jnp.int32, (owners * slots, 1), 0) // slots
    wanted = wanted + jnp.where(((whom ^ me) & side) != 0, float(held), 0.0)
    choose = jnp.where(
        lax.broadcasted_iota(jnp.int32, (owners * slots, 2 * held), 1).astype(F32) == wanted, 1.0, 0.0).astype(BF16)

    for c, (start, size) in enumerate(zip(starts, sizes)):
        cols = pl.ds(start, size)
        lend(c).wait_recv()
        block = dot(choose, table[:, cols])
        sending[:, :, cols] = block.reshape(owners, slots, size).astype(BF16)
        for owner in (me, partner):
            here(sending.at[owner, :, cols], rows.at[owner, :, cols], row_recv.at[c]).start()

        @pl.loop(1, owners - 1, unroll=10)
        def _(i):
            place_of = other(1 + lax.rem(i + owners // 2 - 1, owners - 2))
            away = jnp.where(((me ^ place_of) & side) != 0, way, 0)
            there(sending.at[place_of, :, cols], rows.at[me ^ away, :, cols], row_send.at[0], row_recv.at[c],
                  *split(place_of ^ away)).start()

    def blocks(c):
        return pl.ds(starts[c] // LANES, sizes[c] // LANES)

    def share(c, h, m):
        return lambda n: there(mem.at[h, blocks(c)], mem.at[h, blocks(c)], pass_send.at[0],
                               pass_recv.at[c * (heads - 1) + n - 1], me_p, me_t ^ m)

    def arrived(c, n):
        return there(mem.at[me_t ^ n, blocks(c)], mem.at[me_t ^ n, blocks(c)], pass_send.at[0],
                     pass_recv.at[c * (heads - 1) + n - 1], me_p, me_t ^ n)

    def relayed(c):
        return c != last

    def compact(c):
        cols = pl.ds(starts[c], sizes[c])
        there(sending.at[:, :, cols], rows.at[:, :, cols], row_send.at[0], row_recv.at[c], me_p, me_t).wait_recv()
        mine = dot(place[...], rows[:, :, cols].reshape(owners * slots, sizes[c])).astype(BF16)
        for b in range(sizes[c] // LANES):
            mem[me_t, starts[c] // LANES + b] = mine[:, b * LANES:(b + 1) * LANES]
        for m in list(range(2, heads)) + [1]:
            if m % 2 == 1 or not relayed(c):
                share(c, me_t, m)(m).start()

    def relay(c):
        if relayed(c):
            for m in range(3, heads, 2):
                arrived(c, m).wait_recv()
                share(c, me_t ^ m, 1)(m ^ 1).start()

    def operand(c, base, count):
        b0, nb = starts[c] // LANES, sizes[c] // LANES
        return jnp.concatenate([mem[base + h, b0 + b] for h in range(count) for b in range(nb)], axis=1)

    def multiply(c, w, acc, base, count):
        x = operand(c, base, count)
        first = heads * starts[c] + base * sizes[c]
        if not isinstance(first, int):
            first = pl.multiple_of(first, LANES)
        depth = pl.ds(first, count * sizes[c])
        for n in range(columns // part):
            cols = pl.ds(n * part, part)
            value = dot(x, w[depth, cols])
            acc[:, cols] = value if c == 0 else acc[:, cols] + value

    def gathered(c):
        for m in range(1, heads):
            if not relayed(c) or m % 2 == 0 or m == 1:
                arrived(c, m).wait_recv()

    for c in range(last + 1):
        compact(c)
        if c >= 2:
            if c == 2:
                here(wk_hbm, wk, local_sem.at[5]).wait()
                here(wv_hbm, wv, local_sem.at[6]).wait()
            gathered(c - 2)
            multiply(c - 2, wk, acc_k, 0, heads)
            multiply(c - 2, wv, acc_v, 0, heads)
        if c >= 1:
            relay(c - 1)
    gathered(last - 1)
    multiply(last - 1, wk, acc_k, 0, heads)

    pair = me_t - lax.rem(me_t, 2)
    arrived(last, 1).wait_recv()
    multiply(last, wk, acc_k, pair, 2)
    for m in range(2, heads, 2):
        arrived(last, m).wait_recv()
        arrived(last, m + 1).wait_recv()
        if m + 2 < heads:
            multiply(last, wk, acc_k, pair ^ m, 2)

    key_squares = jnp.zeros((requests, LANES), F32)
    crossing = jnp.zeros((requests, LANES), F32)
    base = pair ^ (heads - 2)
    x = operand(last, base, 2)
    depth = pl.ds(pl.multiple_of(heads * starts[last] + base * sizes[last], LANES), 2 * sizes[last])
    for n in range(columns // part):
        key = acc_k[:, n * part:(n + 1) * part] + dot(x, wk[depth, n * part:(n + 1) * part])
        for b in range(part // LANES):
            one = key[:, b * LANES:(b + 1) * LANES]
            key_squares += one * one
            crossing += scaled[:, n * part + b * LANES:n * part + (b + 1) * LANES] * one
    key_squares = jnp.sum(key_squares, axis=1, keepdims=True)
    crossing = jnp.sum(crossing, axis=1, keepdims=True)
    lanes = lax.broadcasted_iota(jnp.int32, (requests, LANES), 1)
    packed = jnp.where(lanes == 0, hidden_squares, jnp.where(lanes == 1, key_squares,
                       jnp.where(lanes == 2, crossing, 0.0)))
    stats[0] = packed.T[:8]
    for m in range(heads - 1, 0, -1):
        there(stats.at[0], stats.at[m], stat_send.at[0], stat_recv.at[0], me_p, me_t ^ m).start()

    multiply(last - 1, wv, acc_v, 0, heads)
    multiply(last, wv, acc_v, 0, heads)

    others = there(stats.at[pl.ds(1, heads - 1)], stats.at[pl.ds(1, heads - 1)], stat_send.at[0], stat_recv.at[0],
                   me_p, me_t)
    others.wait_recv()
    summed = stats[0]
    for m in range(1, heads):
        summed += stats[m]
    hidden_total, key_total, cross_total = summed[0:1], summed[1:2], summed[2:3]
    agreement = (cross_total * lax.rsqrt(hidden_total / model + epsilon)
                 * lax.rsqrt(key_total / model + epsilon))
    gate = jax.nn.sigmoid(agreement / math.sqrt(model))
    gate = jnp.broadcast_to(gate, (LANES, requests)).T
    for c in range(columns // LANES):
        cols = slice(c * LANES, (c + 1) * LANES)
        out_ref[:, cols] = (hidden[:, cols].astype(F32) + gate * acc_v[:, cols]).astype(BF16)

    some = pl.ds(0, owners - 2)
    there(lists_out.at[some], lists_in.at[some], list_send.at[0], list_recv.at[0], me_p, me_t).wait_send()
    there(sending.at[some], rows.at[some], row_send.at[0], row_recv.at[0], me_p, me_t).wait_send()
    there(table.at[pl.ds(0, held)], table.at[pl.ds(held, held)], lend_send.at[0], lend_recv.at[0], me_p, me_t).wait_send()
    few = pl.ds(0, heads - 1)
    there(mem.at[few], mem.at[few], pass_send.at[0], pass_recv.at[0], me_p, me_t).wait_send()
    others.wait_send()


def local(groups, heads, hidden, hash_rows, memory_table, key_weight, value_weight, hidden_gain, key_gain):
    requests, columns = hidden.shape
    held, width = memory_table.shape
    owners = groups * heads
    assert hash_rows.shape[1] == 1 and heads & (heads - 1) == 0 and heads > 1
    assert groups & (groups - 1) == 0 and requests == LANES and groups >= 4 and heads >= 4
    slots = max(8, 2 * max(1, hash_rows.size // owners))
    sizes = []
    left = width - LANES
    while left > 0:
        sizes.append(min(2 * LANES, left))
        left -= sizes[-1]
    sizes.append(LANES)
    any_space = pl.BlockSpec(memory_space=pl.ANY)
    vmem = pl.BlockSpec(memory_space=pltpu.VMEM)
    dma = pltpu.SemaphoreType.DMA
    return pl.pallas_call(
        functools.partial(kernel, groups, heads, slots, tuple(sizes)),
        out_shape=jax.ShapeDtypeStruct((requests, columns), BF16),
        in_specs=[any_space] * 7,
        out_specs=vmem,
        scratch_shapes=[
            pltpu.VMEM((1, 1, requests), jnp.int32),
            pltpu.VMEM((columns,), F32),
            pltpu.VMEM((columns,), F32),
            pltpu.VMEM((2 * held, width), BF16),
            pltpu.VMEM((requests, columns), BF16),
            pltpu.VMEM((requests, columns), F32),
            pltpu.VMEM((heads * width, columns), BF16),
            pltpu.VMEM((heads * width, columns), BF16),
            pltpu.VMEM((owners, 1, LANES), F32),
            pltpu.VMEM((owners, 1, LANES), F32),
            pltpu.VMEM((owners, slots, width), BF16),
            pltpu.VMEM((owners, slots, width), BF16),
            pltpu.VMEM((requests, owners * slots), BF16),
            pltpu.VMEM((heads, width // LANES, requests, LANES), BF16),
            pltpu.VMEM((requests, columns), F32),
            pltpu.VMEM((requests, columns), F32),
            pltpu.VMEM((heads, 8, requests), F32),
            dma((7,)), dma((1,)), dma((1,)), dma((1,)), dma((len(sizes),)),
            dma((1,)), dma((len(sizes) * (heads - 1),)), dma((1,)), dma((1,)),
            dma((1,)), dma((len(sizes),)),
        ],
        compiler_params=pltpu.CompilerParams(
            collective_id=0, has_side_effects=True, vmem_limit_bytes=44 * 1024 * 1024),
    )(*(pltpu.with_memory_space_constraint(x, pltpu.HBM) for x in (
        hash_rows.reshape(1, 1, requests), hidden_gain, key_gain, memory_table, hidden, key_weight, value_weight)))


def solution(mesh):
    return jax.shard_map(
        functools.partial(local, mesh.shape["dp"], mesh.shape["tensor"]),
        mesh=mesh,
        in_specs=(
            P("dp", "tensor"),
            P("dp", "tensor"),
            P(("dp", "tensor"), None),
            P(None, "tensor"),
            P(None, "tensor"),
            P("tensor"),
            P("tensor"),
        ),
        out_specs=P("dp", "tensor"),
        check_vma=False,
    )
```
